32 devices in a mesh: dp: 4 (over z), context: 4 (over y, x), tensor: 2 (over core).
Axes of the slice: x: 2, y: 2, z: 4, core: 2. Of those that a mesh axis runs over, the one named last changes fastest.
Arguments:
- tokens: bfloat16 [4, 4096, 768], P('dp', 'context'), may hold values from -6 to 6
- prefix_length: int32 [4], P('dp'), may hold values from 409 to 2048
- cluster_order: int32 [4, 12, 4096], P('dp', 'tensor'), may hold values from 0 to 4095, as said below
- query_weight: bfloat16 [768, 768], P('dp', 'tensor'), may hold values from -0.3125 to 0.3125
- key_weight: bfloat16 [768, 768], P('dp', 'tensor'), may hold values from -0.3125 to 0.3125
- value_weight: bfloat16 [768, 768], P('dp', 'tensor'), may hold values from -0.21875 to 0.21875
- output_weight: bfloat16 [768, 768], P('tensor', 'dp'), may hold values from -0.625 to 0.625
- inner_weight: bfloat16 [768, 3072], P('dp', 'tensor'), may hold values from -0.21875 to 0.21875
- outer_weight: bfloat16 [3072, 768], P('tensor', 'dp'), may hold values from -0.109375 to 0.109375
- query_bias: float32 [768], P('tensor'), may hold values from -3 to 3
- value_bias: float32 [768], P('tensor'), may hold values from -3 to 3
- output_bias: float32 [768], replicated, may hold values from -2 to 2
- inner_bias: float32 [3072], P('tensor'), may hold values from -3 to 3
- outer_bias: float32 [768], replicated, may hold values from -2 to 2
- first_gain: float32 [768], replicated, may hold values from 0.5 to 1.5
- first_shift: float32 [768], replicated, may hold values from -2 to 2
- second_gain: float32 [768], replicated, may hold values from 0.5 to 1.5
- second_shift: float32 [768], replicated, may hold values from -2 to 2
- cotangent: bfloat16 [4, 4096, 768], P('dp', 'context'), may hold values from -6 to 6
Outputs:
- activations: bfloat16 [4, 4096, 768], P('dp', 'context')
- input_grad: bfloat16 [4, 4096, 768], P('dp', 'context')
- query_weight_grad: float32 [768, 768], P('dp', 'tensor')
- key_weight_grad: float32 [768, 768], P('dp', 'tensor')
- value_weight_grad: float32 [768, 768], P('dp', 'tensor')
- output_weight_grad: float32 [768, 768], P('tensor', 'dp')
- inner_weight_grad: float32 [768, 3072], P('dp', 'tensor')
- outer_weight_grad: float32 [3072, 768], P('tensor', 'dp')
- query_bias_grad: float32 [768], P('tensor')
- value_bias_grad: float32 [768], P('tensor')
- output_bias_grad: float32 [768], replicated
- inner_bias_grad: float32 [3072], P('tensor')
- outer_bias_grad: float32 [768], replicated
- first_gain_grad: float32 [768], replicated
- first_shift_grad: float32 [768], replicated
- second_gain_grad: float32 [768], replicated
- second_shift_grad: float32 [768], replicated
The draws below stay inside these ranges and needn't reach their ends.
Inputs may be any that keep to these rules, and one draw needn't show every extreme that they name: `cluster_order`: the positions of a sequence form pieces of 1024: piece c is c * 1024 to (c + 1) * 1024 - 1. For each sequence and head the entries are a permutation of 0 to 4095, and the entry at slot k * 128 + c * 32 + r, with r < 32, lies in piece c.
All inputs are finite; a program needn't handle non-finite values.
Results may differ from the reference program's by a relative error of at most 0.02.
Values may be sent and summed in bfloat16 or wider, within the bound.
A program may use at most 128 MiB of HBM per device.

```python
import jax
import jax.numpy as jnp
from jax import lax

D = 768
HEADS = 12
HEAD_DIM = 64
FF = 3072
CLUSTER = 128
SLAB = 1024
SEQ_LEN = 4096
SEQS = 4
SHARE = 32
N_TENSOR = 2


def draw_cluster_order(key, part):
    pieces = SEQ_LEN // SLAB
    groups = SEQ_LEN // CLUSTER

    def shuffled(single_key):
        return jax.random.permutation(single_key, SLAB).astype(jnp.int32)
    keys_all = jax.random.split(key, SEQS * HEADS * pieces)
    orders = jax.vmap(shuffled)(keys_all)
    orders = orders.reshape(SEQS, HEADS, pieces, groups, SHARE)
    offsets = (jnp.arange(pieces, dtype=jnp.int32) * SLAB)[None, None, :, None, None]
    orders = orders + offsets
    return jnp.transpose(orders, (0, 1, 3, 2, 4)).reshape(SEQS, HEADS, SEQ_LEN).astype(jnp.int32)


def place_ends(entries, rng, low, largest):
    dims = entries.shape
    spot = [jax.random.randint(jax.random.fold_in(rng, axis), (), 0, dims[axis]) for axis in range(len(dims))]
    entries = entries.at[tuple(spot)].set(low)
    longest = dims.index(max(dims))
    spot[longest] = (spot[longest] + 1) % dims[longest]
    return entries.at[tuple(spot)].set(largest)


def spiked(entries, key, source, target, blocks, factor):
    owner, partner = [(jnp.arange(entries.shape[position]) // (entries.shape[position] // blocks)).reshape([-1 if axis == position else 1 for axis in range(entries.ndim)]) for position in (source, target)]
    chosen = jax.random.permutation(key, blocks)[partner]
    strong = (owner == chosen) | (owner == (partner + blocks // 2) % blocks)
    return jnp.where(strong, factor * entries, entries)


def levels(rng, dims, cuts, smallest, high):
    loudness, own = 1.0, jax.random.fold_in(rng, 6)
    for position, blocks in cuts:
        steps = jnp.exp(jax.random.uniform(jax.random.fold_in(own, position), (blocks,), jnp.float32, smallest / len(cuts), high / len(cuts)))
        loudness = loudness * jnp.repeat(steps, dims[position] // blocks).reshape([-1 if axis == position else 1 for axis in range(len(dims))])
    return loudness


def normal_values(rng, extent, scale, limit, cuts=(), kind=jnp.bfloat16):
    values = jax.random.normal(rng, extent, jnp.float32) * scale
    if len(cuts) > 0:
        values = levels(rng, extent, cuts, -0.22, 0.18) * values
    return jnp.clip(values, min=-limit, max=limit).astype(kind)


def heavy_noise(stream_key, dims, scale, bound, cuts, heavy, held_as=jnp.bfloat16):
    values = scale * jax.random.normal(stream_key, dims, jnp.float32)
    if cuts:
        values = values * levels(stream_key, dims, cuts, -0.22, 0.18)
    return jnp.clip(spiked(values, jax.random.fold_in(stream_key, 3), *heavy), -bound, bound).astype(held_as)


def setup_inputs(seed: int = 0) -> dict:
    splits = jax.random.split(jax.random.key(seed), 20)
    return {
        "tokens": normal_values(splits[0], (SEQS, SEQ_LEN, D), 1.0, 6.0, ((0, 4), (1, 4))),
        "prefix_length": place_ends(jax.random.randint(splits[1], (SEQS,), SEQ_LEN // 10, SEQ_LEN // 2 + 1), jax.random.fold_in(splits[1], 1), SEQ_LEN // 10, (SEQ_LEN // 2 + 1) - 1).astype(jnp.int32),
        "cluster_order": draw_cluster_order(jax.random.fold_in(splits[19], 71), 0),
        "query_weight": normal_values(splits[3], (D, D), (D // 2) ** -0.5, 0.3125, ((0, 4), (1, 2))),
        "key_weight": normal_values(splits[4], (D, D), (D // 2) ** -0.5, 0.3125, ((0, 4), (1, 2))),
        "value_weight": normal_values(splits[5], (D, D), D ** -0.5, 0.21875, ((0, 4), (1, 2))),
        "output_weight": normal_values(splits[6], (D, D), (D // 8) ** -0.5, 0.625, ((0, 2), (1, 4))),
        "inner_weight": normal_values(splits[7], (D, FF), D ** -0.5, 0.21875, ((0, 4), (1, 2))),
        "outer_weight": normal_values(splits[8], (FF, D), FF ** -0.5, 0.109375, ((0, 2), (1, 4))),
        "query_bias": normal_values(splits[9], (D,), 0.5, 3.0, ((0, 2),), jnp.float32),
        "value_bias": normal_values(splits[10], (D,), 0.5, 3.0, ((0, 2),), jnp.float32),
        "output_bias": normal_values(splits[11], (D,), 0.3, 2.0, (), jnp.float32),
        "inner_bias": normal_values(splits[12], (FF,), 0.5, 3.0, ((0, 2),), jnp.float32),
        "outer_bias": normal_values(splits[13], (D,), 0.3, 2.0, (), jnp.float32),
        "first_gain": jnp.clip(1.0 + 0.1 * jax.random.normal(splits[14], (D,), jnp.float32), 0.5, 1.5),
        "first_shift": normal_values(splits[15], (D,), 0.3, 2.0, (), jnp.float32),
        "second_gain": jnp.clip(1.0 + 0.1 * jax.random.normal(splits[16], (D,), jnp.float32), 0.5, 1.5),
        "second_shift": normal_values(splits[17], (D,), 0.3, 2.0, (), jnp.float32),
        "cotangent": heavy_noise(splits[18], (SEQS, SEQ_LEN, D), 1.0, 6.0, ((0, 4), (1, 4)), (0, 2, 4, 2.0)),
    }


@jax.custom_vjp
def low(v):
    return lax.optimization_barrier(v.astype(jnp.bfloat16)).astype(jnp.float32)

@jax.custom_vjp
def low_back(v):
    return v

def low_keep(v):
    return (low(v), None)

def low_pass(kept, grad):
    return (grad,)

def back_keep(v):
    return (v, None)

def back_low(kept, grad):
    return (low(grad),)
low.defvjp(low_keep, low_pass)
low_back.defvjp(back_keep, back_low)
exact_precision = lax.Precision.HIGHEST
norm_epsilon = 1e-12
masked_score = -1e+30

def matmul(left, right):
    return jnp.dot(left, right, precision=exact_precision, preferred_element_type=jnp.float32)

def layer_norm(values, gain, shift):
    center = values - lax.optimization_barrier(jnp.mean(values, axis=-1, keepdims=True))
    spread = lax.optimization_barrier(jnp.mean(center * center, axis=-1, keepdims=True))
    return center * lax.rsqrt(spread + norm_epsilon) * gain + shift

def cluster_attend(query_all, key_all, value_all, prefix, ordering):
    score_scale = HEAD_DIM ** (-0.5)
    groups = SEQ_LEN // CLUSTER

    def grouped(values_in):
        heads_first = jnp.transpose(values_in.reshape(SEQ_LEN, HEADS, HEAD_DIM), (1, 0, 2))
        picked = jnp.take_along_axis(heads_first, ordering[:, :, None], axis=1)
        return picked.reshape(HEADS, groups, CLUSTER, HEAD_DIM)
    grouped_query = grouped(query_all)
    grouped_key = grouped(key_all)
    grouped_value = grouped(value_all)
    places = ordering.reshape(HEADS, groups, CLUSTER)
    scores = low_back(jnp.einsum('hcqd,hckd->hcqk', grouped_query, grouped_key, precision=exact_precision))
    allowed = jnp.logical_or(places[:, :, None, :] <= places[:, :, :, None], places[:, :, None, :] < prefix)
    scores = jnp.where(allowed, scores * score_scale, masked_score)
    row_max = lax.optimization_barrier(jnp.max(scores, axis=-1, keepdims=True))
    exponent = jnp.exp(scores - row_max)
    weights = low(exponent / lax.optimization_barrier(jnp.sum(exponent, axis=-1, keepdims=True)))
    mixed_heads = jnp.einsum('hcqk,hckd->hcqd', weights, grouped_value, precision=exact_precision)
    mixed_heads = mixed_heads.reshape(HEADS, SEQ_LEN, HEAD_DIM)
    inverse = jnp.argsort(ordering, axis=-1)
    restored = jnp.take_along_axis(mixed_heads, inverse[:, :, None], axis=1)
    return jnp.transpose(restored, (1, 0, 2)).reshape(SEQ_LEN, D)

def encoder_layer(sequence_rows, query_weight, key_weight, value_weight, output_weight, inner_weight, outer_weight, query_bias, value_bias, output_bias, inner_bias, outer_bias, first_gain, first_shift, second_gain, second_shift, prefix, ordering):
    head_columns = D // N_TENSOR
    unit_columns = FF // N_TENSOR
    queries, key_parts, values = ([], [], [])
    for section in range(N_TENSOR):
        columns = slice(section * head_columns, (section + 1) * head_columns)
        source = low_back(sequence_rows)
        queries.append(low_back(low(matmul(source, query_weight[:, columns]) + query_bias[columns])))
        key_parts.append(low_back(low(matmul(source, key_weight[:, columns]))))
        values.append(low_back(low(matmul(source, value_weight[:, columns]) + value_bias[columns])))
    query_all = jnp.concatenate(queries, axis=1)
    key_all = jnp.concatenate(key_parts, axis=1)
    value_all = jnp.concatenate(values, axis=1)
    mixed_rows = low_back(low(cluster_attend(query_all, key_all, value_all, prefix, ordering)))
    branch = output_bias
    for section in range(N_TENSOR):
        columns = slice(section * head_columns, (section + 1) * head_columns)
        branch = branch + low(matmul(mixed_rows[:, columns], output_weight[columns, :]))
    branch = low_back(branch)
    first_norm = layer_norm(sequence_rows + branch, first_gain, first_shift)
    first_low = low(first_norm)
    feed_out = outer_bias
    for section in range(N_TENSOR):
        columns = slice(section * unit_columns, (section + 1) * unit_columns)
        inner_pre = low_back(matmul(low_back(first_low), inner_weight[:, columns]) + inner_bias[columns])
        activated = low(jax.nn.gelu(inner_pre, approximate=False))
        feed_out = feed_out + low(matmul(activated, outer_weight[columns, :]))
    feed_out = low_back(feed_out)
    return layer_norm(first_norm + feed_out, second_gain, second_shift)

def reference(tokens, prefix_length, cluster_order, query_weight, key_weight, value_weight, output_weight, inner_weight, outer_weight, query_bias, value_bias, output_bias, inner_bias, outer_bias, first_gain, first_shift, second_gain, second_shift, cotangent):
    params = tuple((param.astype(jnp.float32) for param in (query_weight, key_weight, value_weight, output_weight, inner_weight, outer_weight, query_bias, value_bias, output_bias, inner_bias, outer_bias, first_gain, first_shift, second_gain, second_shift)))

    def one_sequence(totals, inputs):
        sequence_rows, prefix, ordering, tangent = inputs

        def forward(rows_in, *weights):
            return encoder_layer(rows_in, *weights, prefix, ordering)
        result, pullback = jax.vjp(forward, sequence_rows.astype(jnp.float32), *params)
        gradients = pullback(tangent.astype(jnp.float32))
        new_totals = tuple((total + grad_part for total, grad_part in zip(totals, gradients[1:])))
        return (new_totals, (result.astype(jnp.bfloat16), gradients[0].astype(jnp.bfloat16)))
    zeros = tuple((jnp.zeros_like(param) for param in params))
    totals, outputs = lax.scan(one_sequence, zeros, (tokens, prefix_length, cluster_order, cotangent))
    return (outputs[0], outputs[1], totals[0], totals[1], totals[2], totals[3], totals[4], totals[5], totals[6], totals[7], totals[8], totals[9], totals[10], totals[11], totals[12], totals[13], totals[14])
```

```python
import functools

import jax
import jax.numpy as jnp
from jax import lax
from jax.experimental import pallas as pl
from jax.experimental.pallas import tpu as pltpu
from jax.sharding import PartitionSpec as P

HEAD_DIM = 64
CLUSTER = 128


norm_epsilon = 1e-12
masked_score = -1e30


def normalize(values):
    center = values - jnp.mean(values, axis=-1, keepdims=True)
    inverse_root = lax.rsqrt(jnp.mean(center * center, axis=-1, keepdims=True) + norm_epsilon)
    return (center * inverse_root, inverse_root)


def norm_backward(upstream, normed, inverse_root, gain):
    scaled = upstream * gain
    centered = scaled - jnp.mean(scaled, axis=-1, keepdims=True)
    return inverse_root * (centered - normed * jnp.mean(scaled * normed, axis=-1, keepdims=True))


def gelu_slope(inner_pre):
    normal_cdf = 0.5 * (1.0 + lax.erf(inner_pre * 0.7071067811865476))
    return normal_cdf + inner_pre * jnp.exp(-0.5 * inner_pre * inner_pre) * 0.3989422804014327


MESH = pl.DeviceIdType.MESH
BF16 = jnp.bfloat16
F32 = jnp.float32
PAIR = 2 * HEAD_DIM


def dot(a, b):
    return lax.dot_general(a, b, (((1,), (0,)), ((), ())), preferred_element_type=F32)


def dot_nt(a, b):
    return lax.dot_general(a, b, (((1,), (1,)), ((), ())), preferred_element_type=F32)


def dot_tn(a, b):
    return lax.dot_general(a, b, (((0,), (0,)), ((), ())), preferred_element_type=F32)


def remote(src, dst, send_sem, recv_sem, axis, index):
    return pltpu.make_async_remote_copy(
        src_ref=src,
        dst_ref=dst,
        send_sem=send_sem,
        recv_sem=recv_sem,
        device_id={axis: index},
        device_id_type=MESH,
    )


def meet(axes):
    barrier = pltpu.get_barrier_semaphore()
    count = 0
    for axis in axes:
        size, own = lax.axis_size(axis), lax.axis_index(axis)
        for step in range(1, size):
            pl.semaphore_signal(
                barrier,
                inc=1,
                device_id={axis: lax.rem(own + step, size)},
                device_id_type=MESH,
            )
            count += 1
    pl.semaphore_wait(barrier, count)


def low_lanes(shape):
    return lax.broadcasted_iota(jnp.int32, shape, 1) < HEAD_DIM


def one_hot(left, right):
    return jnp.where(left == right, 1.0, 0.0).astype(BF16)


def stack_pair(pair):
    low = low_lanes(pair.shape)
    zero = jnp.zeros_like(pair)
    return jnp.concatenate((jnp.where(low, pair, zero), jnp.where(low, zero, pair)), axis=0)


def fold_pair(stacked):
    rows = stacked.shape[0] // 2
    top, bottom = stacked[:rows], stacked[rows:]
    return jnp.where(low_lanes(top.shape), top, bottom)


def pair_scores(query2, key, mask2):
    raw = dot_nt(query2, key) * HEAD_DIM ** (-0.5)
    return jnp.where(mask2, raw, masked_score)


def pair_mask(cols_ref, rows_ref, pair, group, heads):
    row = pl.multiple_of(group * CLUSTER, CLUSTER)
    parts = []
    for head in (2 * pair, 2 * pair + 1):
        limit = cols_ref[pl.ds(row, CLUSTER), 8 + head : 9 + head]
        place = rows_ref[8 + head : 9 + head, pl.ds(row, CLUSTER)]
        parts.append(place <= limit)
    return parts


def forward_kernel(
    sizes,
    x_ref,
    query_ref,
    key_ref,
    value_ref,
    output_ref,
    inner_ref,
    outer_ref,
    cols_ref,
    rows_ref,
    query_bias_ref,
    value_bias_ref,
    output_bias_ref,
    first_in_ref,
    mixed_ref,
    got_ref,
    proj_ref,
    inner_full_ref,
    outer_full_ref,
    packed,
    sending,
    answer,
    returned,
    part,
    partner_part,
    own_sem,
    gather_send,
    forward_send,
    gather_recv,
    feed_send,
    feed_recv,
    move_send,
    move_recv,
    back_send,
    back_recv,
    pair_send,
    pair_recv,
):
    n_dp, n_ctx, pairs, gathers = sizes
    slab, width = x_ref.shape
    columns = pairs * PAIR
    dp, ctx, core = lax.axis_index("dp"), lax.axis_index("context"), lax.axis_index("tensor")
    chunk = slab // n_ctx
    groups = slab // CLUSTER
    share = CLUSTER // n_ctx
    shard = width // n_dp
    meet(("dp", "context", "tensor") if gathers else ("context", "tensor"))

    own_rows = pl.ds(pl.multiple_of(dp * shard, 16) if gathers else 0, shard)
    feed_copies = []
    if gathers:
        own = []
        for number, source in enumerate((query_ref, key_ref, value_ref, output_ref)):
            own.append(
                pltpu.make_async_copy(
                    source,
                    proj_ref.at[own_rows, pl.ds(number * columns, columns)],
                    own_sem.at[number],
                )
            )
        own.append(pltpu.make_async_copy(inner_ref, inner_full_ref.at[own_rows], own_sem.at[4]))
        own.append(pltpu.make_async_copy(outer_ref, outer_full_ref.at[own_rows], own_sem.at[5]))
        for copy in own:
            copy.start()

        def block(rows_of, block_number):
            rows = pl.ds(pl.multiple_of(rows_of * shard, 16), shard)
            lanes = pl.ds(pl.multiple_of(block_number * columns, columns), columns)
            return proj_ref.at[rows, lanes]

        for copy in own[:4]:
            copy.wait()
        gather_copies = []
        for step in range(1, n_dp):
            copy = remote(
                block(dp, ctx),
                block(dp, ctx),
                gather_send.at[step],
                gather_recv.at[ctx, dp],
                "dp",
                lax.rem(dp + step, n_dp),
            )
            copy.start()
            gather_copies.append(copy)
        for number, (source, full) in enumerate(
            ((inner_ref, inner_full_ref), (outer_ref, outer_full_ref))
        ):
            for step in range(1, n_dp):
                copy = remote(
                    source,
                    full.at[own_rows],
                    feed_send.at[number, step],
                    feed_recv.at[number, dp],
                    "dp",
                    lax.rem(dp + step, n_dp),
                )
                copy.start()
                feed_copies.append(copy)
        for step in range(1, n_dp):
            source = lax.rem(dp - step + n_dp, n_dp)
            remote(
                block(source, ctx),
                block(source, ctx),
                gather_send.at[step],
                gather_recv.at[ctx, source],
                "dp",
                source,
            ).wait_recv()
            for hop in range(1, n_ctx):
                copy = remote(
                    block(source, ctx),
                    block(source, ctx),
                    forward_send.at[step, hop],
                    gather_recv.at[ctx, source],
                    "context",
                    lax.rem(ctx + hop, n_ctx),
                )
                copy.start()
                gather_copies.append(copy)
        for hop in range(1, n_ctx):
            other = lax.rem(ctx - hop + n_ctx, n_ctx)
            for step in range(1, n_dp):
                source = lax.rem(dp - step + n_dp, n_dp)
                remote(
                    block(source, other),
                    block(source, other),
                    forward_send.at[step, hop],
                    gather_recv.at[other, source],
                    "context",
                    other,
                ).wait_recv()
    else:
        for number, source in enumerate((query_ref, key_ref, value_ref, output_ref)):
            proj_ref[:, number * columns : (number + 1) * columns] = source[...]

    def project(step, carry):
        rows = pl.ds(pl.multiple_of(step * chunk, chunk), chunk)
        values = dot(x_ref[rows, :], proj_ref[:, : 3 * columns])
        low = low_lanes((chunk, PAIR))
        for pair in range(pairs):
            lanes = slice(pair * PAIR, (pair + 1) * PAIR)
            query = values[:, lanes] + query_bias_ref[:, lanes]
            key = values[:, columns + pair * PAIR : columns + (pair + 1) * PAIR]
            value = (
                values[:, 2 * columns + pair * PAIR : 2 * columns + (pair + 1) * PAIR]
                + value_bias_ref[:, lanes]
            )
            first = jnp.where(low, query, pltpu.roll(key, HEAD_DIM, 1))
            second = jnp.where(low, pltpu.roll(query, HEAD_DIM, 1), key)
            packed[pair, rows, 0:PAIR] = first.astype(BF16)
            packed[pair, rows, PAIR : 2 * PAIR] = second.astype(BF16)
            packed[pair, rows, 2 * PAIR : 3 * PAIR] = value.astype(BF16)
        return carry

    lax.fori_loop(0, n_ctx, project, 0)

    own_share = pl.ds(pl.multiple_of(ctx * share, share), share)

    def pick(pair, target):
        rows = pl.ds(pl.multiple_of(target * chunk, chunk), chunk)
        positions = lax.broadcasted_iota(jnp.int32, (chunk, slab), 1)
        tables = [
            one_hot(cols_ref[rows, head : head + 1], positions) for head in (2 * pair, 2 * pair + 1)
        ]
        shared = packed[pair, :, 2 * PAIR : 3 * PAIR]
        even = dot(tables[0], jnp.concatenate((packed[pair, :, 0:PAIR], shared), axis=1))
        odd = dot(tables[1], jnp.concatenate((packed[pair, :, PAIR : 2 * PAIR], shared), axis=1))
        low = low_lanes((chunk, PAIR))
        query = jnp.where(low, even[:, :PAIR], pltpu.roll(odd[:, :PAIR], HEAD_DIM, 1))
        key = jnp.where(low, pltpu.roll(even[:, :PAIR], HEAD_DIM, 1), odd[:, :PAIR])
        value = jnp.where(low, even[:, PAIR:], odd[:, PAIR:])
        for number, piece in enumerate((query, key, value)):
            sending[pair, target, :, :, number * PAIR : (number + 1) * PAIR] = piece.astype(
                BF16
            ).reshape(groups, share, PAIR)

    def moved(pair, hop):
        target = lax.rem(ctx + hop, n_ctx)
        source = sending.at[pair, target]
        landing = got_ref.at[pair, :, own_share, :]
        if hop == 0:
            return pltpu.make_async_copy(source, landing, move_recv.at[pair, 0])
        return remote(
            source, landing, move_send.at[pair, hop], move_recv.at[pair, hop], "context", target
        )

    for pair in range(pairs):
        for hop in (*range(1, n_ctx), 0):
            pick(pair, lax.rem(ctx + hop, n_ctx))
            moved(pair, hop).start()

    def sent_back(pair, hop):
        target = lax.rem(ctx - hop + n_ctx, n_ctx)
        rows = pl.ds(pl.multiple_of(target * share, share), share)
        source = answer.at[pair, :, rows, :]
        landing = returned.at[pair, ctx]
        if hop == 0:
            return pltpu.make_async_copy(source, landing, back_recv.at[pair, 0])
        return remote(
            source, landing, back_send.at[pair, hop], back_recv.at[pair, hop], "context", target
        )

    for pair in range(pairs):
        for hop in range(n_ctx):
            copy = moved(pair, hop)
            if hop == 0:
                copy.wait()
            else:
                copy.wait_recv()

        def attend(group, carry):
            query2 = stack_pair(got_ref[pair, group, :, 0:PAIR])
            key = got_ref[pair, group, :, PAIR : 2 * PAIR]
            value = got_ref[pair, group, :, 2 * PAIR : 3 * PAIR]
            masks = pair_mask(cols_ref, rows_ref, pair, group, 2 * pairs)
            raw = dot_nt(query2, key) * HEAD_DIM ** (-0.5)
            scores = jnp.concatenate(
                [
                    jnp.where(mask, raw[i * CLUSTER : (i + 1) * CLUSTER], masked_score)
                    for i, mask in enumerate(masks)
                ],
                axis=0,
            )
            exponent = jnp.exp(scores - jnp.max(scores, axis=1, keepdims=True))
            total = jnp.sum(exponent, axis=1, keepdims=True)
            weights = (exponent / total).astype(BF16)
            answer[pair, group] = fold_pair(dot(weights, value)).astype(BF16)
            return carry

        lax.fori_loop(0, groups, attend, 0, unroll=2)
        for hop in (*range(1, n_ctx), 0):
            sent_back(pair, hop).start()

    for pair in range(pairs):
        for hop in range(n_ctx):
            copy = sent_back(pair, hop)
            if hop == 0:
                copy.wait()
            else:
                copy.wait_recv()

        def restore(step, carry):
            rows = pl.ds(pl.multiple_of(step * chunk, chunk), chunk)
            positions = lax.broadcasted_iota(jnp.int32, (chunk, slab), 0) + step * chunk
            values = returned[pair].reshape(slab, PAIR)
            even = dot(one_hot(rows_ref[2 * pair : 2 * pair + 1, :], positions), values)
            odd = dot(one_hot(rows_ref[2 * pair + 1 : 2 * pair + 2, :], positions), values)
            mixed_ref[rows, pair * PAIR : (pair + 1) * PAIR] = jnp.where(
                low_lanes(even.shape), even, odd
            ).astype(BF16)
            return carry

        lax.fori_loop(0, n_ctx, restore, 0)

    def exchange(step):
        rows = pl.ds(step * chunk, chunk)
        return remote(
            part.at[rows],
            partner_part.at[rows],
            pair_send.at[step],
            pair_recv.at[step],
            "tensor",
            1 - core,
        )

    for step in range(n_ctx):
        rows = slice(step * chunk, (step + 1) * chunk)
        part[rows, :] = dot_nt(mixed_ref[rows, :], proj_ref[:, 3 * columns :]).astype(BF16)
        exchange(step).start()
    for step in range(n_ctx):
        rows = slice(step * chunk, (step + 1) * chunk)
        exchange(step).wait_recv()
        branch = part[rows, :].astype(F32) + partner_part[rows, :].astype(F32)
        first_in_ref[rows, :] = x_ref[rows, :].astype(F32) + (branch + output_bias_ref[...])

    for step in range(n_ctx):
        exchange(step).wait_send()
    for pair in range(pairs):
        for hop in range(1, n_ctx):
            moved(pair, hop).wait_send()
            sent_back(pair, hop).wait_send()
    if gathers:
        for copy in gather_copies:
            copy.wait_send()
        for copy in feed_copies:
            copy.wait_send()
        for number, full in enumerate((inner_full_ref, outer_full_ref)):
            own[4 + number].wait()
            for step in range(1, n_dp):
                source = lax.rem(dp - step + n_dp, n_dp)
                rows = pl.ds(pl.multiple_of(source * shard, 16), shard)
                remote(
                    full.at[rows],
                    full.at[rows],
                    feed_send.at[number, step],
                    feed_recv.at[number, source],
                    "dp",
                    source,
                ).wait_recv()


def forward_attention(x, weights, cols, rows, biases, gathers):
    n_dp, n_ctx = lax.axis_size("dp"), lax.axis_size("context")
    slab, width = x.shape
    columns = weights[0].shape[1]
    hidden = weights[4].shape[1]
    pairs = columns // PAIR
    groups, share, chunk = slab // CLUSTER, CLUSTER // n_ctx, slab // n_ctx
    vmem = pl.BlockSpec(memory_space=pltpu.VMEM)
    hbm = pl.BlockSpec(memory_space=pl.ANY)
    dma = pltpu.SemaphoreType.DMA
    shapes = (
        jax.ShapeDtypeStruct((slab, width), F32),
        jax.ShapeDtypeStruct((slab, columns), BF16),
        jax.ShapeDtypeStruct((pairs, groups, CLUSTER, 3 * PAIR), BF16),
        jax.ShapeDtypeStruct((width, 4 * columns), BF16),
        jax.ShapeDtypeStruct((width, hidden), BF16),
        jax.ShapeDtypeStruct((width, hidden), BF16),
    )
    weight_spec = hbm if gathers else vmem
    return pl.pallas_call(
        functools.partial(forward_kernel, (n_dp, n_ctx, pairs, gathers)),
        out_shape=shapes,
        in_specs=[vmem] + [weight_spec] * 4 + [hbm] * 2 + [vmem] * 5,
        out_specs=(vmem, vmem, vmem, vmem, hbm, hbm),
        scratch_shapes=[
            pltpu.VMEM((pairs, slab, 3 * PAIR), BF16),
            pltpu.VMEM((pairs, n_ctx, groups, share, 3 * PAIR), BF16),
            pltpu.VMEM((pairs, groups, CLUSTER, PAIR), BF16),
            pltpu.VMEM((pairs, n_ctx, groups, share, PAIR), BF16),
            pltpu.VMEM((slab, width), BF16),
            pltpu.VMEM((slab, width), BF16),
            dma((6,)),
            dma((n_dp,)),
            dma((n_dp, n_ctx)),
            dma((4, n_dp)),
            dma((2, n_dp)),
            dma((2, n_dp)),
            dma((pairs, n_ctx)),
            dma((pairs, n_ctx)),
            dma((pairs, n_ctx)),
            dma((pairs, n_ctx)),
            dma((n_ctx,)),
            dma((n_ctx,)),
        ],
        compiler_params=pltpu.CompilerParams(collective_id=0, has_side_effects=True),
        name="forward_attention",
    )(x, *weights, cols, rows, *biases)


def token_sum(values):
    return jnp.sum(values.astype(F32), axis=0)


def slot_tables(cluster_order, prefix_length, own, n_ctx):
    heads, length = cluster_order.shape[1:]
    slab = length // n_ctx
    order = cluster_order.reshape(heads, n_ctx, slab // CLUSTER, n_ctx, CLUSTER // n_ctx)
    rows = lax.dynamic_index_in_dim(order, own, axis=3, keepdims=False).reshape(heads, slab)
    rows = rows - own * slab
    places = lax.dynamic_slice_in_dim(cluster_order[0], own * slab, slab, axis=1)
    gap = jnp.zeros((8 - heads % 8, slab), jnp.int32)
    limits = jnp.maximum(places, prefix_length[0] - 1)
    along = jnp.concatenate((rows, gap, places, gap), axis=0)
    down = jnp.concatenate((rows, gap, limits, gap), axis=0).T
    return down, along


def permute_rows(values, rows, backward):
    slab = values.shape[1]
    positions = lax.broadcasted_iota(jnp.int32, (1, slab), 1)

    def one_head(pair):
        head_values, head_rows = pair
        table = (head_rows[:, None] == positions).astype(BF16)
        return (dot_tn if backward else dot)(table, head_values).astype(BF16)

    return lax.map(one_head, (values, rows))


def swap(values):
    return lax.all_to_all(values, "context", split_axis=0, concat_axis=0, tiled=True)


def shards(
    tokens,
    prefix_length,
    cluster_order,
    query_weight,
    key_weight,
    value_weight,
    output_weight,
    inner_weight,
    outer_weight,
    query_bias,
    value_bias,
    output_bias,
    inner_bias,
    outer_bias,
    first_gain,
    first_shift,
    second_gain,
    second_shift,
    cotangent,
):
    n_dp, n_ctx = lax.axis_size("dp"), lax.axis_size("context")
    own = lax.axis_index("context")
    x, upstream = tokens[0], cotangent[0].astype(F32)
    slab, width = x.shape
    gathers = query_weight.shape[0] % 16 == 0
    weights = (query_weight, key_weight, value_weight, output_weight.T, inner_weight, outer_weight.T)
    if not gathers:
        weights = tuple(lax.all_gather(w, "dp", axis=0, tiled=True) for w in weights)
    columns = query_weight.shape[1]
    heads = columns // HEAD_DIM
    pairs = heads // 2
    groups, share = slab // CLUSTER, CLUSTER // n_ctx
    cols, rows = slot_tables(cluster_order, prefix_length, own, n_ctx)
    biases = (query_bias[None], value_bias[None], output_bias[None])
    first_in, mixed, got, proj, inner_full, outer_full = forward_attention(
        x, weights, cols, rows, biases, gathers
    )
    if not gathers:
        inner_full, outer_full = weights[4:]
    first_normed, first_root = normalize(first_in)
    first_norm = first_normed * first_gain + first_shift
    first_low = first_norm.astype(BF16)
    inner_pre = dot(first_low, inner_full) + inner_bias
    activated = jax.nn.gelu(inner_pre, approximate=False).astype(BF16)
    feed_part = dot_nt(activated, outer_full)
    feed_out = lax.psum(feed_part.astype(BF16), "tensor").astype(F32) + outer_bias
    second_normed, second_root = normalize(first_norm + feed_out)
    activations = (second_normed * second_gain + second_shift).astype(BF16)
    second_gain_grad = token_sum(upstream * second_normed)
    second_shift_grad = token_sum(upstream)
    second_in_grad = norm_backward(upstream, second_normed, second_root, second_gain)
    feed_grad = second_in_grad.astype(BF16)
    outer_bias_grad = token_sum(feed_grad)
    outer_weight_grad = dot_tn(feed_grad, activated)
    act_grad = dot(feed_grad, outer_full)
    inner_grad = (act_grad * gelu_slope(inner_pre)).astype(BF16)
    inner_bias_grad = token_sum(inner_grad)
    inner_weight_grad = dot_tn(first_low, inner_grad)
    first_part = dot_nt(inner_grad, inner_full)
    first_grad = second_in_grad + lax.psum(first_part.astype(BF16), "tensor").astype(F32)
    first_gain_grad = token_sum(first_grad * first_normed)
    first_shift_grad = token_sum(first_grad)
    summed_grad = norm_backward(first_grad, first_normed, first_root, first_gain)
    branch_grad = summed_grad.astype(BF16)
    output_bias_grad = token_sum(branch_grad)
    output_weight_grad = dot_tn(branch_grad, mixed)
    mixed_grad = dot(branch_grad, proj[:, 3 * columns :]).astype(BF16)

    head_rows = rows[:heads]
    picked = permute_rows(mixed_grad.reshape(slab, heads, HEAD_DIM).transpose(1, 0, 2), head_rows, False)
    picked = picked.reshape(heads, n_ctx, groups, share, HEAD_DIM).transpose(1, 0, 2, 3, 4)
    got_grad = swap(picked).transpose(1, 2, 0, 3, 4).reshape(heads, groups, CLUSTER, HEAD_DIM)
    parts = got.reshape(pairs, groups, CLUSTER, 3, 2, HEAD_DIM).transpose(3, 0, 4, 1, 2, 5)
    query, key, value = parts.reshape(3, heads, groups, CLUSTER, HEAD_DIM)
    allowed = (
        rows[8 : 8 + heads].reshape(heads, groups, 1, CLUSTER)
        <= cols.T[8 : 8 + heads].reshape(heads, groups, CLUSTER, 1)
    )
    scores = jnp.einsum("hcqd,hckd->hcqk", query, key, preferred_element_type=F32)
    scores = jnp.where(allowed, scores * HEAD_DIM ** (-0.5), masked_score)
    probs = jax.nn.softmax(scores, axis=-1)
    prob_grad = jnp.einsum("hcqd,hckd->hcqk", got_grad, value, preferred_element_type=F32)
    value_grad = jnp.einsum(
        "hcqk,hcqd->hckd", probs.astype(BF16), got_grad, preferred_element_type=F32
    ).astype(BF16)
    score_grad = (
        probs
        * (prob_grad - jnp.sum(probs * prob_grad, axis=-1, keepdims=True))
        * HEAD_DIM ** (-0.5)
    ).astype(BF16)
    query_grad = jnp.einsum(
        "hcqk,hckd->hcqd", score_grad, key, preferred_element_type=F32
    ).astype(BF16)
    key_grad = jnp.einsum(
        "hcqk,hcqd->hckd", score_grad, query, preferred_element_type=F32
    ).astype(BF16)
    back = jnp.concatenate((query_grad, key_grad, value_grad), axis=3)
    back = back.reshape(heads, groups, n_ctx, share, 3 * HEAD_DIM).transpose(2, 0, 1, 3, 4)
    back = swap(back).transpose(1, 0, 2, 3, 4).reshape(heads, slab, 3 * HEAD_DIM)
    restored = permute_rows(back, head_rows, True)
    restored = restored.reshape(heads, slab, 3, HEAD_DIM).transpose(1, 2, 0, 3).reshape(slab, 3 * columns)
    bias_sums = token_sum(restored)
    query_bias_grad, value_bias_grad = bias_sums[:columns], bias_sums[2 * columns :]
    proj_weight_grad = dot_tn(x, restored)
    input_part = dot_nt(restored, proj[:, : 3 * columns])
    input_grad = (
        summed_grad + lax.psum(input_part.astype(BF16), "tensor").astype(F32)
    ).astype(BF16)
    small_sums = lax.psum(
        (
            query_bias_grad,
            value_bias_grad,
            output_bias_grad,
            inner_bias_grad,
            outer_bias_grad,
            first_gain_grad,
            first_shift_grad,
            second_gain_grad,
            second_shift_grad,
        ),
        ("dp", "context"),
    )

    def reduced(grad):
        piece = lax.psum_scatter(grad.astype(BF16), "dp", scatter_dimension=0, tiled=True)
        return lax.psum(piece, "context").astype(F32)

    proj_owned = reduced(proj_weight_grad)
    return (
        activations[None],
        input_grad[None],
        proj_owned[:, :columns],
        proj_owned[:, columns : 2 * columns],
        proj_owned[:, 2 * columns :],
        reduced(output_weight_grad).T,
        reduced(inner_weight_grad),
        reduced(outer_weight_grad).T,
        *small_sums,
    )


def solution(mesh):
    placed = (
        P("dp", "context", None),
        P("dp"),
        P("dp", "tensor", None),
        P("dp", "tensor"),
        P("dp", "tensor"),
        P("dp", "tensor"),
        P("tensor", "dp"),
        P("dp", "tensor"),
        P("tensor", "dp"),
        P("tensor"),
        P("tensor"),
        P(),
        P("tensor"),
        P(),
        P(),
        P(),
        P(),
        P(),
        P("dp", "context", None),
    )
    return jax.shard_map(
        shards,
        mesh=mesh,
        in_specs=placed,
        out_specs=(
            P("dp", "context", None),
            P("dp", "context", None),
            P("dp", "tensor"),
            P("dp", "tensor"),
            P("dp", "tensor"),
            P("tensor", "dp"),
            P("dp", "tensor"),
            P("tensor", "dp"),
            P("tensor"),
            P("tensor"),
            P(),
            P("tensor"),
            P(),
            P(),
            P(),
            P(),
            P(),
        ),
        check_vma=False,
    )
```

```python
import functools

import jax
import jax.numpy as jnp
from jax import lax
from jax.experimental import pallas as pl
from jax.experimental.pallas import tpu as pltpu
from jax.sharding import PartitionSpec as P

HEAD_DIM = 64
CLUSTER = 128


norm_epsilon = 1e-12
masked_score = -1e30


def normalize(values):
    center = values - jnp.mean(values, axis=-1, keepdims=True)
    inverse_root = lax.rsqrt(jnp.mean(center * center, axis=-1, keepdims=True) + norm_epsilon)
    return (center * inverse_root, inverse_root)


def norm_backward(upstream, normed, inverse_root, gain):
    scaled = upstream * gain
    centered = scaled - jnp.mean(scaled, axis=-1, keepdims=True)
    return inverse_root * (centered - normed * jnp.mean(scaled * normed, axis=-1, keepdims=True))


MESH = pl.DeviceIdType.MESH
BF16 = jnp.bfloat16
F32 = jnp.float32
PAIR = 2 * HEAD_DIM


def dot(a, b):
    return lax.dot_general(a, b, (((1,), (0,)), ((), ())), preferred_element_type=F32)


def dot_nt(a, b):
    return lax.dot_general(a, b, (((1,), (1,)), ((), ())), preferred_element_type=F32)


def dot_tn(a, b):
    return lax.dot_general(a, b, (((0,), (0,)), ((), ())), preferred_element_type=F32)


def remote(src, dst, send_sem, recv_sem, axis, index):
    return pltpu.make_async_remote_copy(
        src_ref=src,
        dst_ref=dst,
        send_sem=send_sem,
        recv_sem=recv_sem,
        device_id={axis: index},
        device_id_type=MESH,
    )


def meet(axes):
    barrier = pltpu.get_barrier_semaphore()
    count = 0
    for axis in axes:
        size, own = lax.axis_size(axis), lax.axis_index(axis)
        for step in range(1, size):
            pl.semaphore_signal(
                barrier,
                inc=1,
                device_id={axis: lax.rem(own + step, size)},
                device_id_type=MESH,
            )
            count += 1
    pl.semaphore_wait(barrier, count)


def low_lanes(shape):
    return lax.broadcasted_iota(jnp.int32, shape, 1) < HEAD_DIM


def one_hot(left, right):
    return jnp.where(left == right, 1.0, 0.0).astype(BF16)


def stack_pair(pair):
    low = low_lanes(pair.shape)
    zero = jnp.zeros_like(pair)
    return jnp.concatenate((jnp.where(low, pair, zero), jnp.where(low, zero, pair)), axis=0)


def fold_pair(stacked):
    rows = stacked.shape[0] // 2
    top, bottom = stacked[:rows], stacked[rows:]
    return jnp.where(low_lanes(top.shape), top, bottom)


def pair_scores(query2, key, mask2):
    raw = dot_nt(query2, key) * HEAD_DIM ** (-0.5)
    return jnp.where(mask2, raw, masked_score)


def pair_mask(cols_ref, rows_ref, pair, group, heads):
    row = pl.multiple_of(group * CLUSTER, CLUSTER)
    parts = []
    for head in (2 * pair, 2 * pair + 1):
        limit = cols_ref[pl.ds(row, CLUSTER), 8 + head : 9 + head]
        place = rows_ref[8 + head : 9 + head, pl.ds(row, CLUSTER)]
        parts.append(place <= limit)
    return parts


def forward_kernel(
    sizes,
    x_ref,
    query_ref,
    key_ref,
    value_ref,
    output_ref,
    inner_ref,
    outer_ref,
    cols_ref,
    rows_ref,
    query_bias_ref,
    value_bias_ref,
    output_bias_ref,
    first_in_ref,
    mixed_ref,
    got_ref,
    proj_ref,
    inner_full_ref,
    outer_full_ref,
    packed,
    sending,
    answer,
    returned,
    part,
    partner_part,
    own_sem,
    gather_send,
    forward_send,
    gather_recv,
    feed_send,
    feed_recv,
    move_send,
    move_recv,
    back_send,
    back_recv,
    pair_send,
    pair_recv,
):
    n_dp, n_ctx, pairs, gathers = sizes
    slab, width = x_ref.shape
    columns = pairs * PAIR
    dp, ctx, core = lax.axis_index("dp"), lax.axis_index("context"), lax.axis_index("tensor")
    chunk = slab // n_ctx
    groups = slab // CLUSTER
    share = CLUSTER // n_ctx
    shard = width // n_dp
    meet(("dp", "context", "tensor") if gathers else ("context", "tensor"))

    own_rows = pl.ds(pl.multiple_of(dp * shard, 16) if gathers else 0, shard)
    feed_copies = []
    if gathers:
        own = []
        for number, source in enumerate((query_ref, key_ref, value_ref, output_ref)):
            own.append(
                pltpu.make_async_copy(
                    source,
                    proj_ref.at[own_rows, pl.ds(number * columns, columns)],
                    own_sem.at[number],
                )
            )
        own.append(pltpu.make_async_copy(inner_ref, inner_full_ref.at[own_rows], own_sem.at[4]))
        own.append(pltpu.make_async_copy(outer_ref, outer_full_ref.at[own_rows], own_sem.at[5]))
        for copy in own:
            copy.start()

        def block(rows_of, block_number):
            rows = pl.ds(pl.multiple_of(rows_of * shard, 16), shard)
            lanes = pl.ds(pl.multiple_of(block_number * columns, columns), columns)
            return proj_ref.at[rows, lanes]

        for copy in own[:4]:
            copy.wait()
        gather_copies = []
        for step in range(1, n_dp):
            copy = remote(
                block(dp, ctx),
                block(dp, ctx),
                gather_send.at[step],
                gather_recv.at[ctx, dp],
                "dp",
                lax.rem(dp + step, n_dp),
            )
            copy.start()
            gather_copies.append(copy)
        for number, (source, full) in enumerate(
            ((inner_ref, inner_full_ref), (outer_ref, outer_full_ref))
        ):
            for step in range(1, n_dp):
                copy = remote(
                    source,
                    full.at[own_rows],
                    feed_send.at[number, step],
                    feed_recv.at[number, dp],
                    "dp",
                    lax.rem(dp + step, n_dp),
                )
                copy.start()
                feed_copies.append(copy)
        for step in range(1, n_dp):
            source = lax.rem(dp - step + n_dp, n_dp)
            remote(
                block(source, ctx),
                block(source, ctx),
                gather_send.at[step],
                gather_recv.at[ctx, source],
                "dp",
                source,
            ).wait_recv()
            for hop in range(1, n_ctx):
                copy = remote(
                    block(source, ctx),
                    block(source, ctx),
                    forward_send.at[step, hop],
                    gather_recv.at[ctx, source],
                    "context",
                    lax.rem(ctx + hop, n_ctx),
                )
                copy.start()
                gather_copies.append(copy)
        for hop in range(1, n_ctx):
            other = lax.rem(ctx - hop + n_ctx, n_ctx)
            for step in range(1, n_dp):
                source = lax.rem(dp - step + n_dp, n_dp)
                remote(
                    block(source, other),
                    block(source, other),
                    forward_send.at[step, hop],
                    gather_recv.at[other, source],
                    "context",
                    other,
                ).wait_recv()
    else:
        for number, source in enumerate((query_ref, key_ref, value_ref, output_ref)):
            proj_ref[:, number * columns : (number + 1) * columns] = source[...]

    def project(step, carry):
        rows = pl.ds(pl.multiple_of(step * chunk, chunk), chunk)
        values = dot(x_ref[rows, :], proj_ref[:, : 3 * columns])
        low = low_lanes((chunk, PAIR))
        for pair in range(pairs):
            lanes = slice(pair * PAIR, (pair + 1) * PAIR)
            query = values[:, lanes] + query_bias_ref[:, lanes]
            key = values[:, columns + pair * PAIR : columns + (pair + 1) * PAIR]
            value = (
                values[:, 2 * columns + pair * PAIR : 2 * columns + (pair + 1) * PAIR]
                + value_bias_ref[:, lanes]
            )
            first = jnp.where(low, query, pltpu.roll(key, HEAD_DIM, 1))
            second = jnp.where(low, pltpu.roll(query, HEAD_DIM, 1), key)
            packed[pair, rows, 0:PAIR] = first.astype(BF16)
            packed[pair, rows, PAIR : 2 * PAIR] = second.astype(BF16)
            packed[pair, rows, 2 * PAIR : 3 * PAIR] = value.astype(BF16)
        return carry

    lax.fori_loop(0, n_ctx, project, 0)

    own_share = pl.ds(pl.multiple_of(ctx * share, share), share)

    def pick(pair, target):
        rows = pl.ds(pl.multiple_of(target * chunk, chunk), chunk)
        positions = lax.broadcasted_iota(jnp.int32, (chunk, slab), 1)
        tables = [
            one_hot(cols_ref[rows, head : head + 1], positions) for head in (2 * pair, 2 * pair + 1)
        ]
        shared = packed[pair, :, 2 * PAIR : 3 * PAIR]
        even = dot(tables[0], jnp.concatenate((packed[pair, :, 0:PAIR], shared), axis=1))
        odd = dot(tables[1], jnp.concatenate((packed[pair, :, PAIR : 2 * PAIR], shared), axis=1))
        low = low_lanes((chunk, PAIR))
        query = jnp.where(low, even[:, :PAIR], pltpu.roll(odd[:, :PAIR], HEAD_DIM, 1))
        key = jnp.where(low, pltpu.roll(even[:, :PAIR], HEAD_DIM, 1), odd[:, :PAIR])
        value = jnp.where(low, even[:, PAIR:], odd[:, PAIR:])
        for number, piece in enumerate((query, key, value)):
            sending[pair, target, :, :, number * PAIR : (number + 1) * PAIR] = piece.astype(
                BF16
            ).reshape(groups, share, PAIR)

    def moved(pair, hop):
        target = lax.rem(ctx + hop, n_ctx)
        source = sending.at[pair, target]
        landing = got_ref.at[pair, :, own_share, :]
        if hop == 0:
            return pltpu.make_async_copy(source, landing, move_recv.at[pair, 0])
        return remote(
            source, landing, move_send.at[pair, hop], move_recv.at[pair, hop], "context", target
        )

    for pair in range(pairs):
        for hop in (*range(1, n_ctx), 0):
            pick(pair, lax.rem(ctx + hop, n_ctx))
            moved(pair, hop).start()

    def sent_back(pair, hop):
        target = lax.rem(ctx - hop + n_ctx, n_ctx)
        rows = pl.ds(pl.multiple_of(target * share, share), share)
        source = answer.at[pair, :, rows, :]
        landing = returned.at[pair, ctx]
        if hop == 0:
            return pltpu.make_async_copy(source, landing, back_recv.at[pair, 0])
        return remote(
            source, landing, back_send.at[pair, hop], back_recv.at[pair, hop], "context", target
        )

    for pair in range(pairs):
        for hop in range(n_ctx):
            copy = moved(pair, hop)
            if hop == 0:
                copy.wait()
            else:
                copy.wait_recv()

        def attend(group, carry):
            query2 = stack_pair(got_ref[pair, group, :, 0:PAIR])
            key = got_ref[pair, group, :, PAIR : 2 * PAIR]
            value = got_ref[pair, group, :, 2 * PAIR : 3 * PAIR]
            masks = pair_mask(cols_ref, rows_ref, pair, group, 2 * pairs)
            raw = dot_nt(query2, key) * HEAD_DIM ** (-0.5)
            scores = jnp.concatenate(
                [
                    jnp.where(mask, raw[i * CLUSTER : (i + 1) * CLUSTER], masked_score)
                    for i, mask in enumerate(masks)
                ],
                axis=0,
            )
            exponent = jnp.exp(scores - jnp.max(scores, axis=1, keepdims=True))
            total = jnp.sum(exponent, axis=1, keepdims=True)
            weights = (exponent / total).astype(BF16)
            answer[pair, group] = fold_pair(dot(weights, value)).astype(BF16)
            return carry

        lax.fori_loop(0, groups, attend, 0, unroll=2)
        for hop in (*range(1, n_ctx), 0):
            sent_back(pair, hop).start()

    for pair in range(pairs):
        for hop in range(n_ctx):
            copy = sent_back(pair, hop)
            if hop == 0:
                copy.wait()
            else:
                copy.wait_recv()

        def restore(step, carry):
            rows = pl.ds(pl.multiple_of(step * chunk, chunk), chunk)
            positions = lax.broadcasted_iota(jnp.int32, (chunk, slab), 0) + step * chunk
            values = returned[pair].reshape(slab, PAIR)
            even = dot(one_hot(rows_ref[2 * pair : 2 * pair + 1, :], positions), values)
            odd = dot(one_hot(rows_ref[2 * pair + 1 : 2 * pair + 2, :], positions), values)
            mixed_ref[rows, pair * PAIR : (pair + 1) * PAIR] = jnp.where(
                low_lanes(even.shape), even, odd
            ).astype(BF16)
            return carry

        lax.fori_loop(0, n_ctx, restore, 0)

    def exchange(step):
        rows = pl.ds(step * chunk, chunk)
        return remote(
            part.at[rows],
            partner_part.at[rows],
            pair_send.at[step],
            pair_recv.at[step],
            "tensor",
            1 - core,
        )

    for step in range(n_ctx):
        rows = slice(step * chunk, (step + 1) * chunk)
        part[rows, :] = dot_nt(mixed_ref[rows, :], proj_ref[:, 3 * columns :]).astype(BF16)
        exchange(step).start()
    for step in range(n_ctx):
        rows = slice(step * chunk, (step + 1) * chunk)
        exchange(step).wait_recv()
        branch = part[rows, :].astype(F32) + partner_part[rows, :].astype(F32)
        first_in_ref[rows, :] = x_ref[rows, :].astype(F32) + (branch + output_bias_ref[...])

    for step in range(n_ctx):
        exchange(step).wait_send()
    for pair in range(pairs):
        for hop in range(1, n_ctx):
            moved(pair, hop).wait_send()
            sent_back(pair, hop).wait_send()
    if gathers:
        for copy in gather_copies:
            copy.wait_send()
        for copy in feed_copies:
            copy.wait_send()
        for number, full in enumerate((inner_full_ref, outer_full_ref)):
            own[4 + number].wait()
            for step in range(1, n_dp):
                source = lax.rem(dp - step + n_dp, n_dp)
                rows = pl.ds(pl.multiple_of(source * shard, 16), shard)
                remote(
                    full.at[rows],
                    full.at[rows],
                    feed_send.at[number, step],
                    feed_recv.at[number, source],
                    "dp",
                    source,
                ).wait_recv()


def forward_attention(x, weights, cols, rows, biases, gathers):
    n_dp, n_ctx = lax.axis_size("dp"), lax.axis_size("context")
    slab, width = x.shape
    columns = weights[0].shape[1]
    hidden = weights[4].shape[1]
    pairs = columns // PAIR
    groups, share, chunk = slab // CLUSTER, CLUSTER // n_ctx, slab // n_ctx
    vmem = pl.BlockSpec(memory_space=pltpu.VMEM)
    hbm = pl.BlockSpec(memory_space=pl.ANY)
    dma = pltpu.SemaphoreType.DMA
    shapes = (
        jax.ShapeDtypeStruct((slab, width), F32),
        jax.ShapeDtypeStruct((slab, columns), BF16),
        jax.ShapeDtypeStruct((pairs, groups, CLUSTER, 3 * PAIR), BF16),
        jax.ShapeDtypeStruct((width, 4 * columns), BF16),
        jax.ShapeDtypeStruct((width, hidden), BF16),
        jax.ShapeDtypeStruct((width, hidden), BF16),
    )
    weight_spec = hbm if gathers else vmem
    return pl.pallas_call(
        functools.partial(forward_kernel, (n_dp, n_ctx, pairs, gathers)),
        out_shape=shapes,
        in_specs=[vmem] + [weight_spec] * 4 + [hbm] * 2 + [vmem] * 5,
        out_specs=(vmem, vmem, vmem, vmem, hbm, hbm),
        scratch_shapes=[
            pltpu.VMEM((pairs, slab, 3 * PAIR), BF16),
            pltpu.VMEM((pairs, n_ctx, groups, share, 3 * PAIR), BF16),
            pltpu.VMEM((pairs, groups, CLUSTER, PAIR), BF16),
            pltpu.VMEM((pairs, n_ctx, groups, share, PAIR), BF16),
            pltpu.VMEM((slab, width), BF16),
            pltpu.VMEM((slab, width), BF16),
            dma((6,)),
            dma((n_dp,)),
            dma((n_dp, n_ctx)),
            dma((4, n_dp)),
            dma((2, n_dp)),
            dma((2, n_dp)),
            dma((pairs, n_ctx)),
            dma((pairs, n_ctx)),
            dma((pairs, n_ctx)),
            dma((pairs, n_ctx)),
            dma((n_ctx,)),
            dma((n_ctx,)),
        ],
        compiler_params=pltpu.CompilerParams(collective_id=0, has_side_effects=True),
        name="forward_attention",
    )(x, *weights, cols, rows, *biases)


def sublane_sums(values):
    rows, width = values.shape
    return jnp.sum(values.reshape(rows // 8, 8, width), axis=0)


def feed_kernel(
    blocks,
    first_in_ref,
    cotangent_ref,
    inner_ref,
    outer_ref,
    inner_bias_ref,
    outer_bias_ref,
    first_gain_ref,
    first_shift_ref,
    second_gain_ref,
    second_shift_ref,
    activations_ref,
    summed_ref,
    branch_ref,
    inner_grad_ref,
    outer_grad_ref,
    sums_ref,
    low,
    first,
    act,
    slope,
    feed,
    part,
    partner_part,
    sums,
    pair_send,
    pair_recv,
):
    slab, width = first_in_ref.shape
    hidden = inner_ref.shape[1]
    chunk = slab // blocks
    core = lax.axis_index("tensor")
    meet(("tensor",))
    sums[...] = jnp.zeros_like(sums)

    def rows_of(step):
        return pl.ds(pl.multiple_of(step * chunk, chunk), chunk)

    def exchange(stage, step):
        return remote(
            part.at[stage, rows_of(step)],
            partner_part.at[stage, rows_of(step)],
            pair_send.at[stage, step],
            pair_recv.at[stage, step],
            "tensor",
            1 - core,
        )

    def expand(step, carry):
        rows = rows_of(step)
        normed, _ = normalize(first_in_ref[rows, :])
        values = normed * first_gain_ref[...] + first_shift_ref[...]
        first[rows, :] = values
        low[rows, :] = values.astype(BF16)
        inner = dot(low[rows, :], inner_ref[...]) + inner_bias_ref[...]
        cdf = 0.5 * (1.0 + lax.erf(inner * 0.7071067811865476))
        act[rows, :] = (inner * cdf).astype(BF16)
        slope[rows, :] = (
            cdf + inner * jnp.exp(-0.5 * inner * inner) * 0.3989422804014327
        ).astype(BF16)
        part[0, rows, :] = dot_nt(act[rows, :], outer_ref[...]).astype(BF16)
        exchange(0, step).start()
        return carry

    lax.fori_loop(0, blocks, expand, 0)

    def turn(step, carry):
        rows = rows_of(step)
        exchange(0, step).wait_recv()
        out = part[0, rows, :].astype(F32) + partner_part[0, rows, :].astype(F32)
        normed, root = normalize(first[rows, :] + (out + outer_bias_ref[...]))
        activations_ref[rows, :] = (
            normed * second_gain_ref[...] + second_shift_ref[...]
        ).astype(BF16)
        upstream = cotangent_ref[rows, :].astype(F32)
        grad = norm_backward(upstream, normed, root, second_gain_ref[...])
        first[rows, :] = grad
        rounded = grad.astype(BF16)
        feed[rows, :] = rounded
        sums[2] += sublane_sums(rounded.astype(F32))
        sums[5] += sublane_sums(upstream * normed)
        sums[6] += sublane_sums(upstream)
        inner_grad = dot(rounded, outer_ref[...]) * slope[rows, :].astype(F32)
        slope[rows, :] = inner_grad.astype(BF16)
        inner_sums = sublane_sums(slope[rows, :].astype(F32))
        sums[0] += inner_sums[:, :width]
        sums[1] += inner_sums[:, width:]
        part[1, rows, :] = dot_nt(slope[rows, :], inner_ref[...]).astype(BF16)
        exchange(1, step).start()
        return carry

    lax.fori_loop(0, blocks, turn, 0)

    strip = hidden // blocks

    def weigh(step, carry):
        lanes = pl.ds(pl.multiple_of(step * strip, strip), strip)
        outer_grad_ref[step] = dot_tn(feed[...], act[:, lanes]).astype(BF16)
        inner_grad_ref[step] = dot_tn(low[...], slope[:, lanes]).astype(BF16)
        return carry

    lax.fori_loop(0, blocks, weigh, 0)

    def close(step, carry):
        rows = rows_of(step)
        exchange(1, step).wait_recv()
        back = part[1, rows, :].astype(F32) + partner_part[1, rows, :].astype(F32)
        grad = first[rows, :] + back
        normed, root = normalize(first_in_ref[rows, :])
        sums[3] += sublane_sums(grad * normed)
        sums[4] += sublane_sums(grad)
        summed = norm_backward(grad, normed, root, first_gain_ref[...])
        summed_ref[rows, :] = summed
        rounded = summed.astype(BF16)
        branch_ref[rows, :] = rounded
        sums[7] += sublane_sums(rounded.astype(F32))
        return carry

    lax.fori_loop(0, blocks, close, 0)
    sums_ref[...] = jnp.sum(sums[...], axis=1)

    def finish(step, carry):
        exchange(0, step).wait_send()
        exchange(1, step).wait_send()
        return carry

    lax.fori_loop(0, blocks, finish, 0)


def feed_forward(first_in, cotangent, inner, outer, vectors):
    slab, width = first_in.shape
    hidden = inner.shape[1]
    blocks = lax.axis_size("context")
    vmem = pl.BlockSpec(memory_space=pltpu.VMEM)
    dma = pltpu.SemaphoreType.DMA
    return pl.pallas_call(
        functools.partial(feed_kernel, blocks),
        out_shape=(
            jax.ShapeDtypeStruct((slab, width), BF16),
            jax.ShapeDtypeStruct((slab, width), F32),
            jax.ShapeDtypeStruct((slab, width), BF16),
            jax.ShapeDtypeStruct((blocks, width, hidden // blocks), BF16),
            jax.ShapeDtypeStruct((blocks, width, hidden // blocks), BF16),
            jax.ShapeDtypeStruct((8, width), F32),
        ),
        in_specs=[vmem] * (4 + len(vectors)),
        out_specs=[vmem] * 6,
        scratch_shapes=[
            pltpu.VMEM((slab, width), BF16),
            pltpu.VMEM((slab, width), F32),
            pltpu.VMEM((slab, hidden), BF16),
            pltpu.VMEM((slab, hidden), BF16),
            pltpu.VMEM((slab, width), BF16),
            pltpu.VMEM((2, slab, width), BF16),
            pltpu.VMEM((2, slab, width), BF16),
            pltpu.VMEM((8, 8, width), F32),
            dma((2, blocks)),
            dma((2, blocks)),
        ],
        compiler_params=pltpu.CompilerParams(collective_id=1, has_side_effects=True),
        name="feed_forward",
    )(first_in, cotangent, inner, outer, *vectors)


def backward_kernel(
    sizes,
    x_ref,
    branch_ref,
    summed_ref,
    mixed_ref,
    got_ref,
    proj_ref,
    cols_ref,
    rows_ref,
    inner_part_ref,
    outer_part_ref,
    sums_ref,
    input_grad_ref,
    final_ref,
    totals_ref,
    proj_part_ref,
    upstream,
    sending,
    landed,
    answer,
    returned,
    restored,
    collected,
    pieces,
    scattered,
    part,
    partner_part,
    sums,
    sums_ctx,
    sums_dp,
    move_send,
    move_recv,
    back_send,
    back_recv,
    spread_send,
    spread_recv,
    scatter_send,
    scatter_recv,
    gather_send,
    gather_recv,
    sums_send,
    sums_recv,
    pair_send,
    pair_recv,
):
    n_dp, n_ctx, pairs, reduces = sizes
    slab, width = x_ref.shape
    columns = pairs * PAIR
    dp, ctx, core = lax.axis_index("dp"), lax.axis_index("context"), lax.axis_index("tensor")
    chunk = slab // n_ctx
    groups = slab // CLUSTER
    share = CLUSTER // n_ctx
    shard = width // n_dp
    meet(("dp", "context", "tensor") if reduces else ("context", "tensor"))

    def rows_of(step):
        return pl.ds(pl.multiple_of(step * chunk, chunk), chunk)

    def spread(kind, hop):
        source = (proj_part_ref, inner_part_ref, outer_part_ref)[kind]
        target = lax.rem(ctx + hop, n_ctx)
        if hop == 0:
            return pltpu.make_async_copy(
                source.at[target], collected.at[kind, 0], spread_recv.at[kind, 0]
            )
        return remote(
            source.at[target],
            collected.at[kind, hop],
            spread_send.at[kind, hop],
            spread_recv.at[kind, hop],
            "context",
            target,
        )

    def scatter(kind, step):
        target = lax.rem(dp + step, n_dp)
        rows = pl.ds(pl.multiple_of(target * shard, 16), shard)
        return remote(
            pieces.at[kind, rows],
            scattered.at[kind, step],
            scatter_send.at[kind, step],
            scatter_recv.at[kind, step],
            "dp",
            target,
        )

    def regather(kind, hop, mine):
        owner = ctx if mine else lax.rem(ctx - hop + n_ctx, n_ctx)
        target = lax.rem(ctx + hop, n_ctx)
        return remote(
            final_ref.at[kind, owner],
            final_ref.at[kind, owner],
            gather_send.at[kind, hop],
            gather_recv.at[kind, hop],
            "context",
            target,
        )

    def start_spread(kind):
        for hop in (*range(1, n_ctx), 0):
            spread(kind, hop).start()

    def sum_spread(kind):
        for hop in range(n_ctx):
            copy = spread(kind, hop)
            if hop == 0:
                copy.wait()
            else:
                copy.wait_recv()

        def add(step, carry):
            rows = pl.ds(pl.multiple_of(step * shard, 16), shard)
            total = collected[kind, 0, rows, :].astype(F32)
            for hop in range(1, n_ctx):
                total = total + collected[kind, hop, rows, :].astype(F32)
            pieces[kind, rows, :] = total.astype(BF16)
            return carry

        lax.fori_loop(0, n_dp, add, 0)
        for step in range(1, n_dp):
            scatter(kind, step).start()

    def sum_scatter(kind):
        rows = pl.ds(pl.multiple_of(dp * shard, 16), shard)
        total = pieces[kind, rows, :].astype(F32)
        for step in range(1, n_dp):
            scatter(kind, step).wait_recv()
            total = total + scattered[kind, step].astype(F32)
        final_ref[kind, ctx] = total.astype(BF16)
        for hop in range(1, n_ctx):
            regather(kind, hop, True).start()

    def project(step, carry):
        rows = rows_of(step)
        upstream[rows, :] = dot(branch_ref[rows, :], proj_ref[:, 3 * columns :]).astype(BF16)
        return carry

    lax.fori_loop(0, n_ctx, project, 0)

    own_share = pl.ds(pl.multiple_of(ctx * share, share), share)

    def moved(pair, hop):
        target = lax.rem(ctx + hop, n_ctx)
        source = sending.at[pair, target]
        landing = landed.at[pair, :, own_share, :]
        if hop == 0:
            return pltpu.make_async_copy(source, landing, move_recv.at[pair, 0])
        return remote(
            source, landing, move_send.at[pair, hop], move_recv.at[pair, hop], "context", target
        )

    for pair in range(pairs):
        for hop in (*range(1, n_ctx), 0):
            target = lax.rem(ctx + hop, n_ctx)
            rows = rows_of(target)
            positions = lax.broadcasted_iota(jnp.int32, (chunk, slab), 1)
            values = upstream[:, pair * PAIR : (pair + 1) * PAIR]
            even = dot(one_hot(cols_ref[rows, 2 * pair : 2 * pair + 1], positions), values)
            odd = dot(one_hot(cols_ref[rows, 2 * pair + 1 : 2 * pair + 2], positions), values)
            picked = jnp.where(low_lanes(even.shape), even, odd).astype(BF16)
            sending[pair, target] = picked.reshape(groups, share, PAIR)
            moved(pair, hop).start()

    if reduces:
        start_spread(2)
    for step in range(2):
        rows = slice(step * width // 2, (step + 1) * width // 2)
        proj_part_ref[3, rows, :] = dot_tn(branch_ref[:, rows], mixed_ref[...]).astype(BF16)

    def sent_back(pair, hop):
        target = lax.rem(ctx - hop + n_ctx, n_ctx)
        rows = pl.ds(pl.multiple_of(target * share, share), share)
        source = answer.at[pair, :, rows, :]
        landing = returned.at[pair, ctx]
        if hop == 0:
            return pltpu.make_async_copy(source, landing, back_recv.at[pair, 0])
        return remote(
            source, landing, back_send.at[pair, hop], back_recv.at[pair, hop], "context", target
        )

    for pair in range(pairs):
        for hop in range(n_ctx):
            copy = moved(pair, hop)
            if hop == 0:
                copy.wait()
            else:
                copy.wait_recv()

        def attend(group, carry):
            query2 = stack_pair(got_ref[pair, group, :, 0:PAIR])
            key = got_ref[pair, group, :, PAIR : 2 * PAIR]
            value = got_ref[pair, group, :, 2 * PAIR : 3 * PAIR]
            grad2 = stack_pair(landed[pair, group])
            masks = pair_mask(cols_ref, rows_ref, pair, group, 2 * pairs)
            raw = dot_nt(query2, key) * HEAD_DIM ** (-0.5)
            scores = jnp.concatenate(
                [
                    jnp.where(mask, raw[i * CLUSTER : (i + 1) * CLUSTER], masked_score)
                    for i, mask in enumerate(masks)
                ],
                axis=0,
            )
            exponent = jnp.exp(scores - jnp.max(scores, axis=1, keepdims=True))
            probs = exponent / jnp.sum(exponent, axis=1, keepdims=True)
            prob_grad = dot_nt(grad2, value)
            inner = jnp.sum(probs * prob_grad, axis=1, keepdims=True)
            score_grad = (probs * (prob_grad - inner) * HEAD_DIM ** (-0.5)).astype(BF16)
            value_grad = dot_tn(probs.astype(BF16), grad2)
            query_grad = fold_pair(dot(score_grad, key))
            key_grad = dot_tn(score_grad, query2)
            low = low_lanes((CLUSTER, PAIR))
            first = jnp.where(low, query_grad, pltpu.roll(key_grad, HEAD_DIM, 1))
            second = jnp.where(low, pltpu.roll(query_grad, HEAD_DIM, 1), key_grad)
            answer[pair, group, :, 0:PAIR] = first.astype(BF16)
            answer[pair, group, :, PAIR : 2 * PAIR] = second.astype(BF16)
            answer[pair, group, :, 2 * PAIR : 3 * PAIR] = value_grad.astype(BF16)
            return carry

        lax.fori_loop(0, groups, attend, 0, unroll=2)
        for hop in (*range(1, n_ctx), 0):
            sent_back(pair, hop).start()

    if reduces:
        start_spread(1)
        sum_spread(2)
    for pair in range(pairs):
        for hop in range(n_ctx):
            copy = sent_back(pair, hop)
            if hop == 0:
                copy.wait()
            else:
                copy.wait_recv()

        def restore(step, carry):
            rows = rows_of(step)
            positions = lax.broadcasted_iota(jnp.int32, (chunk, slab), 0) + step * chunk
            values = returned[pair].reshape(slab, 3 * PAIR)
            shared = values[:, 2 * PAIR :]
            even = dot(
                one_hot(rows_ref[2 * pair : 2 * pair + 1, :], positions),
                jnp.concatenate((values[:, :PAIR], shared), axis=1),
            )
            odd = dot(
                one_hot(rows_ref[2 * pair + 1 : 2 * pair + 2, :], positions), values[:, PAIR:]
            )
            low = low_lanes((chunk, PAIR))
            first, second = even[:, :PAIR], odd[:, :PAIR]
            query = jnp.where(low, first, pltpu.roll(second, HEAD_DIM, 1))
            key = jnp.where(low, pltpu.roll(first, HEAD_DIM, 1), second)
            value = jnp.where(low, even[:, PAIR:], odd[:, PAIR:])
            for number, piece in enumerate((query, key, value)):
                lanes = slice(number * columns + pair * PAIR, number * columns + (pair + 1) * PAIR)
                restored[rows, lanes] = piece.astype(BF16)
            return carry

        lax.fori_loop(0, n_ctx, restore, 0)

    for number in range(3):
        lanes = slice(number * columns, (number + 1) * columns)
        proj_part_ref[number] = dot_tn(x_ref[...], restored[:, lanes]).astype(BF16)
    if reduces:
        start_spread(0)

    def exchange(step):
        return remote(
            part.at[rows_of(step)],
            partner_part.at[rows_of(step)],
            pair_send.at[step],
            pair_recv.at[step],
            "tensor",
            1 - core,
        )

    def give(step, carry):
        rows = rows_of(step)
        part[rows, :] = dot_nt(restored[rows, :], proj_ref[:, : 3 * columns]).astype(BF16)
        exchange(step).start()
        return carry

    lax.fori_loop(0, n_ctx, give, 0)

    sums[0:8, :] = sums_ref[...]
    sums[8:16, :] = jnp.zeros((8, width), F32)
    for place, number in enumerate((0, 2)):
        values = restored[:, number * columns : (number + 1) * columns].astype(F32)
        sums[8:9, place * columns : (place + 1) * columns] = jnp.sum(values, axis=0, keepdims=True)

    def sums_out(level, step):
        axis, size, own = (("context", n_ctx, ctx), ("dp", n_dp, dp))[level]
        landing = (sums_ctx, sums_dp)[level]
        return remote(
            sums.at[level * 16 : level * 16 + 16],
            landing.at[own],
            sums_send.at[level, step],
            sums_recv.at[level, step],
            axis,
            lax.rem(own + step, size),
        )

    if reduces:
        for step in range(1, n_ctx):
            sums_out(0, step).start()
        sums_ctx[ctx] = sums[0:16, :]

    def take(step, carry):
        rows = rows_of(step)
        exchange(step).wait_recv()
        back = part[rows, :].astype(F32) + partner_part[rows, :].astype(F32)
        input_grad_ref[rows, :] = (summed_ref[rows, :] + back).astype(BF16)
        return carry

    lax.fori_loop(0, n_ctx, take, 0)

    if reduces:
        sum_scatter(2)
        for step in range(1, n_ctx):
            sums_out(0, step).wait_recv()
        sums[16:32, :] = jnp.sum(sums_ctx[...], axis=0)
        for step in range(1, n_dp):
            sums_out(1, step).start()
        sums_dp[dp] = sums[16:32, :]
        sum_spread(1)
        sum_spread(0)
        for step in range(1, n_dp):
            sums_out(1, step).wait_recv()
        totals_ref[...] = jnp.sum(sums_dp[...], axis=0)
        sum_scatter(1)
        sum_scatter(0)
        for kind in range(3):
            for hop in range(1, n_ctx):
                regather(kind, hop, False).wait_recv()
            for hop in range(1, n_ctx):
                spread(kind, hop).wait_send()
                regather(kind, hop, True).wait_send()
            for step in range(1, n_dp):
                scatter(kind, step).wait_send()
        for level, size in enumerate((n_ctx, n_dp)):
            for step in range(1, size):
                sums_out(level, step).wait_send()
    else:
        totals_ref[...] = sums[0:16, :]
    for step in range(n_ctx):
        exchange(step).wait_send()
    for pair in range(pairs):
        for hop in range(1, n_ctx):
            moved(pair, hop).wait_send()
            sent_back(pair, hop).wait_send()


def backward_attention(
    x, branch, summed, mixed, got, proj, cols, rows, inner_part, outer_part, sums, reduces
):
    n_dp, n_ctx = lax.axis_size("dp"), lax.axis_size("context")
    slab, width = x.shape
    columns = mixed.shape[1]
    pairs = columns // PAIR
    groups, share = slab // CLUSTER, CLUSTER // n_ctx
    shard = width // n_dp
    vmem = pl.BlockSpec(memory_space=pltpu.VMEM)
    hbm = pl.BlockSpec(memory_space=pl.ANY)
    dma = pltpu.SemaphoreType.DMA
    kinds, steps = (3, n_dp) if reduces else (1, 2)
    return pl.pallas_call(
        functools.partial(backward_kernel, (n_dp, n_ctx, pairs, reduces)),
        out_shape=(
            jax.ShapeDtypeStruct((slab, width), BF16),
            jax.ShapeDtypeStruct((kinds, n_ctx, shard, columns), BF16),
            jax.ShapeDtypeStruct((16, width), F32),
            jax.ShapeDtypeStruct((4, width, columns), BF16),
        ),
        in_specs=[vmem] * 8 + [hbm] * 2 + [vmem],
        out_specs=[vmem] * 4,
        scratch_shapes=[
            pltpu.VMEM((slab, columns), BF16),
            pltpu.VMEM((pairs, n_ctx, groups, share, PAIR), BF16),
            pltpu.VMEM((pairs, groups, CLUSTER, PAIR), BF16),
            pltpu.VMEM((pairs, groups, CLUSTER, 3 * PAIR), BF16),
            pltpu.VMEM((pairs, n_ctx, groups, share, 3 * PAIR), BF16),
            pltpu.VMEM((slab, 3 * columns), BF16),
            pltpu.VMEM((kinds, n_ctx, width, columns), BF16),
            pltpu.VMEM((kinds, width, columns), BF16),
            pltpu.VMEM((kinds, steps, shard, columns), BF16),
            pltpu.VMEM((slab, width), BF16),
            pltpu.VMEM((slab, width), BF16),
            pltpu.VMEM((32, width), F32),
            pltpu.VMEM((n_ctx, 16, width), F32),
            pltpu.VMEM((steps, 16, width), F32),
            dma((pairs, n_ctx)),
            dma((pairs, n_ctx)),
            dma((pairs, n_ctx)),
            dma((pairs, n_ctx)),
            dma((kinds, n_ctx)),
            dma((kinds, n_ctx)),
            dma((kinds, steps)),
            dma((kinds, steps)),
            dma((kinds, n_ctx)),
            dma((kinds, n_ctx)),
            dma((2, max(n_ctx, steps))),
            dma((2, max(n_ctx, steps))),
            dma((n_ctx,)),
            dma((n_ctx,)),
        ],
        compiler_params=pltpu.CompilerParams(collective_id=2, has_side_effects=True),
        name="backward_attention",
    )(x, branch, summed, mixed, got, proj, cols, rows, inner_part, outer_part, sums)


def slot_tables(cluster_order, prefix_length, own, n_ctx):
    heads, length = cluster_order.shape[1:]
    slab = length // n_ctx
    order = cluster_order.reshape(heads, n_ctx, slab // CLUSTER, n_ctx, CLUSTER // n_ctx)
    rows = lax.dynamic_index_in_dim(order, own, axis=3, keepdims=False).reshape(heads, slab)
    rows = rows - own * slab
    places = lax.dynamic_slice_in_dim(cluster_order[0], own * slab, slab, axis=1)
    gap = jnp.zeros((8 - heads % 8, slab), jnp.int32)
    limits = jnp.maximum(places, prefix_length[0] - 1)
    along = jnp.concatenate((rows, gap, places, gap), axis=0)
    down = jnp.concatenate((rows, gap, limits, gap), axis=0).T
    return down, along


def shards(
    tokens,
    prefix_length,
    cluster_order,
    query_weight,
    key_weight,
    value_weight,
    output_weight,
    inner_weight,
    outer_weight,
    query_bias,
    value_bias,
    output_bias,
    inner_bias,
    outer_bias,
    first_gain,
    first_shift,
    second_gain,
    second_shift,
    cotangent,
):
    n_ctx = lax.axis_size("context")
    own = lax.axis_index("context")
    x = tokens[0]
    shard, columns = query_weight.shape
    aligned = shard % 16 == 0
    weights = (query_weight, key_weight, value_weight, output_weight.T, inner_weight, outer_weight.T)
    if not aligned:
        weights = tuple(lax.all_gather(w, "dp", axis=0, tiled=True) for w in weights)
    cols, rows = slot_tables(cluster_order, prefix_length, own, n_ctx)
    biases = (query_bias[None], value_bias[None], output_bias[None])
    first_in, mixed, got, proj, inner_full, outer_full = forward_attention(
        x, weights, cols, rows, biases, aligned
    )
    if not aligned:
        inner_full, outer_full = weights[4:]
    vectors = (inner_bias, outer_bias, first_gain, first_shift, second_gain, second_shift)
    activations, summed, branch, inner_part, outer_part, sums = feed_forward(
        first_in, cotangent[0], inner_full, outer_full, tuple(v[None] for v in vectors)
    )
    input_grad, final, totals, proj_part = backward_attention(
        x, branch, summed, mixed, got, proj, cols, rows, inner_part, outer_part, sums, aligned
    )
    if not aligned:
        parts = jnp.stack((proj_part, inner_part, outer_part))
        piece = lax.psum_scatter(parts, "dp", scatter_dimension=2, tiled=True)
        final = lax.psum(piece, "context")
        totals = lax.psum(totals, ("dp", "context"))
    final = final.astype(F32)
    wide = final.transpose(0, 2, 1, 3).reshape(3, shard, n_ctx * columns)
    return (
        activations[None],
        input_grad[None],
        final[0, 0],
        final[0, 1],
        final[0, 2],
        final[0, 3].T,
        wide[1],
        wide[2].T,
        totals[8, :columns],
        totals[8, columns:],
        totals[7],
        totals[0:2].reshape(-1),
        totals[2],
        totals[3],
        totals[4],
        totals[5],
        totals[6],
    )


def solution(mesh):
    placed = (
        P("dp", "context", None),
        P("dp"),
        P("dp", "tensor", None),
        P("dp", "tensor"),
        P("dp", "tensor"),
        P("dp", "tensor"),
        P("tensor", "dp"),
        P("dp", "tensor"),
        P("tensor", "dp"),
        P("tensor"),
        P("tensor"),
        P(),
        P("tensor"),
        P(),
        P(),
        P(),
        P(),
        P(),
        P("dp", "context", None),
    )
    return jax.shard_map(
        shards,
        mesh=mesh,
        in_specs=placed,
        out_specs=(
            P("dp", "context", None),
            P("dp", "context", None),
            P("dp", "tensor"),
            P("dp", "tensor"),
            P("dp", "tensor"),
            P("tensor", "dp"),
            P("dp", "tensor"),
            P("tensor", "dp"),
            P("tensor"),
            P("tensor"),
            P(),
            P("tensor"),
            P(),
            P(),
            P(),
            P(),
            P(),
        ),
        check_vma=False,
    )
```

```python
import functools

import jax
import jax.numpy as jnp
from jax import lax
from jax.experimental import pallas as pl
from jax.experimental.pallas import tpu as pltpu
from jax.sharding import PartitionSpec as P

HEAD_DIM = 64
CLUSTER = 128


norm_epsilon = 1e-12
masked_score = -1e30


def normalize(values):
    center = values - jnp.mean(values, axis=-1, keepdims=True)
    inverse_root = lax.rsqrt(jnp.mean(center * center, axis=-1, keepdims=True) + norm_epsilon)
    return (center * inverse_root, inverse_root)


def norm_backward(upstream, normed, inverse_root, gain):
    scaled = upstream * gain
    centered = scaled - jnp.mean(scaled, axis=-1, keepdims=True)
    return inverse_root * (centered - normed * jnp.mean(scaled * normed, axis=-1, keepdims=True))


MESH = pl.DeviceIdType.MESH
BF16 = jnp.bfloat16
F32 = jnp.float32
PAIR = 2 * HEAD_DIM


def dot(a, b):
    return lax.dot_general(a, b, (((1,), (0,)), ((), ())), preferred_element_type=F32)


def dot_nt(a, b):
    return lax.dot_general(a, b, (((1,), (1,)), ((), ())), preferred_element_type=F32)


def dot_tn(a, b):
    return lax.dot_general(a, b, (((0,), (0,)), ((), ())), preferred_element_type=F32)


def remote(src, dst, send_sem, recv_sem, axis, index):
    return pltpu.make_async_remote_copy(
        src_ref=src,
        dst_ref=dst,
        send_sem=send_sem,
        recv_sem=recv_sem,
        device_id={axis: index},
        device_id_type=MESH,
    )


def meet(axes):
    barrier = pltpu.get_barrier_semaphore()
    count = 0
    for axis in axes:
        size, own = lax.axis_size(axis), lax.axis_index(axis)
        for step in range(1, size):
            pl.semaphore_signal(
                barrier,
                inc=1,
                device_id={axis: lax.rem(own + step, size)},
                device_id_type=MESH,
            )
            count += 1
    pl.semaphore_wait(barrier, count)


def row_of(ref):
    return ref[...].reshape(1, ref.shape[0])


def low_lanes(shape):
    return lax.broadcasted_iota(jnp.int32, shape, 1) < HEAD_DIM


def one_hot(left, right):
    return jnp.where(left == right, 1.0, 0.0).astype(BF16)


def stack_pair(pair):
    low = low_lanes(pair.shape)
    zero = jnp.zeros_like(pair)
    return jnp.concatenate((jnp.where(low, pair, zero), jnp.where(low, zero, pair)), axis=0)


def fold_pair(stacked):
    rows = stacked.shape[0] // 2
    top, bottom = stacked[:rows], stacked[rows:]
    return jnp.where(low_lanes(top.shape), top, bottom)


def pair_scores(query2, key, mask2):
    raw = dot_nt(query2, key) * HEAD_DIM ** (-0.5)
    return jnp.where(mask2, raw, masked_score)


def pair_mask(cols_ref, rows_ref, pair, group, heads):
    row = pl.multiple_of(group * CLUSTER, CLUSTER)
    parts = []
    for head in (2 * pair, 2 * pair + 1):
        limit = cols_ref[pl.ds(row, CLUSTER), 8 + head : 9 + head]
        place = rows_ref[8 + head : 9 + head, pl.ds(row, CLUSTER)]
        parts.append(place <= limit)
    return parts


def forward_kernel(
    sizes,
    x_ref,
    query_ref,
    key_ref,
    value_ref,
    output_ref,
    inner_ref,
    outer_ref,
    cols_ref,
    rows_ref,
    query_bias_ref,
    value_bias_ref,
    output_bias_ref,
    first_in_ref,
    mixed_ref,
    got_ref,
    proj_ref,
    inner_full_ref,
    outer_full_ref,
    packed,
    sending,
    answer,
    returned,
    part,
    partner_part,
    own_sem,
    gather_send,
    forward_send,
    gather_recv,
    feed_send,
    feed_recv,
    inner_send,
    inner_forward,
    inner_recv,
    move_send,
    move_recv,
    back_send,
    back_recv,
    pair_send,
    pair_recv,
):
    n_dp, n_ctx, pairs, gathers = sizes
    slab, width = x_ref.shape
    columns = pairs * PAIR
    dp, ctx, core = lax.axis_index("dp"), lax.axis_index("context"), lax.axis_index("tensor")
    chunk = slab // n_ctx
    groups = slab // CLUSTER
    share = CLUSTER // n_ctx
    shard = width // n_dp
    meet(("dp", "context", "tensor") if gathers else ("context", "tensor"))

    own_rows = pl.ds(pl.multiple_of(dp * shard, 16) if gathers else 0, shard)
    feed_copies = []
    if gathers:
        own = []
        for number, source in enumerate((query_ref, key_ref, value_ref, output_ref)):
            own.append(
                pltpu.make_async_copy(
                    source,
                    proj_ref.at[own_rows, pl.ds(number * columns, columns)],
                    own_sem.at[number],
                )
            )
        own.append(pltpu.make_async_copy(inner_ref, inner_full_ref.at[own_rows], own_sem.at[4]))
        own.append(pltpu.make_async_copy(outer_ref, outer_full_ref.at[own_rows], own_sem.at[5]))
        for copy in own:
            copy.start()

        def block(rows_of, block_number):
            rows = pl.ds(pl.multiple_of(rows_of * shard, 16), shard)
            lanes = pl.ds(pl.multiple_of(block_number * columns, columns), columns)
            return proj_ref.at[rows, lanes]

        for copy in own[:4]:
            copy.wait()
        gather_copies = []
        for step in range(1, n_dp):
            copy = remote(
                block(dp, ctx),
                block(dp, ctx),
                gather_send.at[step],
                gather_recv.at[ctx, dp],
                "dp",
                lax.rem(dp + step, n_dp),
            )
            copy.start()
            gather_copies.append(copy)

        def strip(rows_of, block_number):
            rows = pl.ds(pl.multiple_of(rows_of * shard, 16), shard)
            lanes = pl.ds(pl.multiple_of(block_number * columns, columns), columns)
            return inner_full_ref.at[rows, lanes]

        own_lanes = pl.ds(pl.multiple_of(ctx * columns, columns), columns)
        for step in range(1, n_dp):
            copy = remote(
                inner_ref.at[:, own_lanes],
                strip(dp, ctx),
                inner_send.at[step],
                inner_recv.at[ctx, dp],
                "dp",
                lax.rem(dp + step, n_dp),
            )
            copy.start()
            feed_copies.append(copy)
        for step in range(1, n_dp):
            copy = remote(
                outer_ref,
                outer_full_ref.at[own_rows],
                feed_send.at[step],
                feed_recv.at[dp],
                "dp",
                lax.rem(dp + step, n_dp),
            )
            copy.start()
            feed_copies.append(copy)

        def forward_strip(step):
            source = lax.rem(dp - step + n_dp, n_dp)
            remote(
                strip(source, ctx),
                strip(source, ctx),
                inner_send.at[step],
                inner_recv.at[ctx, source],
                "dp",
                source,
            ).wait_recv()
            for hop in range(1, n_ctx):
                copy = remote(
                    strip(source, ctx),
                    strip(source, ctx),
                    inner_forward.at[step, hop],
                    inner_recv.at[ctx, source],
                    "context",
                    lax.rem(ctx + hop, n_ctx),
                )
                copy.start()
                feed_copies.append(copy)

        for step in range(1, n_dp):
            source = lax.rem(dp - step + n_dp, n_dp)
            remote(
                block(source, ctx),
                block(source, ctx),
                gather_send.at[step],
                gather_recv.at[ctx, source],
                "dp",
                source,
            ).wait_recv()
            for hop in range(1, n_ctx):
                copy = remote(
                    block(source, ctx),
                    block(source, ctx),
                    forward_send.at[step, hop],
                    gather_recv.at[ctx, source],
                    "context",
                    lax.rem(ctx + hop, n_ctx),
                )
                copy.start()
                gather_copies.append(copy)
        for hop in range(1, n_ctx):
            other = lax.rem(ctx - hop + n_ctx, n_ctx)
            for step in range(1, n_dp):
                source = lax.rem(dp - step + n_dp, n_dp)
                remote(
                    block(source, other),
                    block(source, other),
                    forward_send.at[step, hop],
                    gather_recv.at[other, source],
                    "context",
                    other,
                ).wait_recv()
    else:
        for number, source in enumerate((query_ref, key_ref, value_ref, output_ref)):
            proj_ref[:, number * columns : (number + 1) * columns] = source[...]

    query_bias, value_bias = row_of(query_bias_ref), row_of(value_bias_ref)
    output_bias = row_of(output_bias_ref)

    def project(step, carry):
        rows = pl.ds(pl.multiple_of(step * chunk, chunk), chunk)
        values = dot(x_ref[rows, :], proj_ref[:, : 3 * columns])
        low = low_lanes((chunk, PAIR))
        for pair in range(pairs):
            lanes = slice(pair * PAIR, (pair + 1) * PAIR)
            query = values[:, lanes] + query_bias[:, lanes]
            key = values[:, columns + pair * PAIR : columns + (pair + 1) * PAIR]
            value = (
                values[:, 2 * columns + pair * PAIR : 2 * columns + (pair + 1) * PAIR]
                + value_bias[:, lanes]
            )
            first = jnp.where(low, query, pltpu.roll(key, HEAD_DIM, 1))
            second = jnp.where(low, pltpu.roll(query, HEAD_DIM, 1), key)
            packed[pair, rows, 0:PAIR] = first.astype(BF16)
            packed[pair, rows, PAIR : 2 * PAIR] = second.astype(BF16)
            packed[pair, rows, 2 * PAIR : 3 * PAIR] = value.astype(BF16)
        return carry

    if gathers:
        forward_strip(1)
    lax.fori_loop(0, n_ctx, project, 0)

    own_share = pl.ds(pl.multiple_of(ctx * share, share), share)

    def pick(pair, target):
        rows = pl.ds(pl.multiple_of(target * chunk, chunk), chunk)
        positions = lax.broadcasted_iota(jnp.int32, (chunk, slab), 1)
        tables = [
            one_hot(cols_ref[rows, head : head + 1], positions) for head in (2 * pair, 2 * pair + 1)
        ]
        shared = packed[pair, :, 2 * PAIR : 3 * PAIR]
        even = dot(tables[0], jnp.concatenate((packed[pair, :, 0:PAIR], shared), axis=1))
        odd = dot(tables[1], jnp.concatenate((packed[pair, :, PAIR : 2 * PAIR], shared), axis=1))
        low = low_lanes((chunk, PAIR))
        query = jnp.where(low, even[:, :PAIR], pltpu.roll(odd[:, :PAIR], HEAD_DIM, 1))
        key = jnp.where(low, pltpu.roll(even[:, :PAIR], HEAD_DIM, 1), odd[:, :PAIR])
        value = jnp.where(low, even[:, PAIR:], odd[:, PAIR:])
        for number, piece in enumerate((query, key, value)):
            sending[pair, target, :, :, number * PAIR : (number + 1) * PAIR] = piece.astype(
                BF16
            ).reshape(groups, share, PAIR)

    def moved(pair, hop):
        target = lax.rem(ctx + hop, n_ctx)
        source = sending.at[pair, target]
        landing = got_ref.at[pair, :, own_share, :]
        if hop == 0:
            return pltpu.make_async_copy(source, landing, move_recv.at[pair, 0])
        return remote(
            source, landing, move_send.at[pair, hop], move_recv.at[pair, hop], "context", target
        )

    for pair in range(pairs):
        for hop in (*range(1, n_ctx), 0):
            pick(pair, lax.rem(ctx + hop, n_ctx))
            moved(pair, hop).start()

    def sent_back(pair, hop):
        target = lax.rem(ctx - hop + n_ctx, n_ctx)
        rows = pl.ds(pl.multiple_of(target * share, share), share)
        source = answer.at[pair, :, rows, :]
        landing = returned.at[pair, ctx]
        if hop == 0:
            return pltpu.make_async_copy(source, landing, back_recv.at[pair, 0])
        return remote(
            source, landing, back_send.at[pair, hop], back_recv.at[pair, hop], "context", target
        )

    for pair in range(pairs):
        for hop in range(n_ctx):
            copy = moved(pair, hop)
            if hop == 0:
                copy.wait()
            else:
                copy.wait_recv()

        def attend(group, carry):
            query2 = stack_pair(got_ref[pair, group, :, 0:PAIR])
            key = got_ref[pair, group, :, PAIR : 2 * PAIR]
            value = got_ref[pair, group, :, 2 * PAIR : 3 * PAIR]
            masks = pair_mask(cols_ref, rows_ref, pair, group, 2 * pairs)
            raw = dot_nt(query2, key) * HEAD_DIM ** (-0.5)
            scores = jnp.concatenate(
                [
                    jnp.where(mask, raw[i * CLUSTER : (i + 1) * CLUSTER], masked_score)
                    for i, mask in enumerate(masks)
                ],
                axis=0,
            )
            exponent = jnp.exp(scores - jnp.max(scores, axis=1, keepdims=True))
            total = jnp.sum(exponent, axis=1, keepdims=True)
            weights = (exponent / total).astype(BF16)
            answer[pair, group] = fold_pair(dot(weights, value)).astype(BF16)
            return carry

        lax.fori_loop(0, groups, attend, 0, unroll=2)
        for hop in (*range(1, n_ctx), 0):
            sent_back(pair, hop).start()
    if gathers:
        for step in range(2, n_dp):
            forward_strip(step)

    for pair in range(pairs):
        for hop in range(n_ctx):
            copy = sent_back(pair, hop)
            if hop == 0:
                copy.wait()
            else:
                copy.wait_recv()

        def restore(step, carry):
            rows = pl.ds(pl.multiple_of(step * chunk, chunk), chunk)
            positions = lax.broadcasted_iota(jnp.int32, (chunk, slab), 0) + step * chunk
            values = returned[pair].reshape(slab, PAIR)
            even = dot(one_hot(rows_ref[2 * pair : 2 * pair + 1, :], positions), values)
            odd = dot(one_hot(rows_ref[2 * pair + 1 : 2 * pair + 2, :], positions), values)
            mixed_ref[rows, pair * PAIR : (pair + 1) * PAIR] = jnp.where(
                low_lanes(even.shape), even, odd
            ).astype(BF16)
            return carry

        lax.fori_loop(0, n_ctx, restore, 0)

    def exchange(step):
        rows = pl.ds(step * chunk, chunk)
        return remote(
            part.at[rows],
            partner_part.at[rows],
            pair_send.at[step],
            pair_recv.at[step],
            "tensor",
            1 - core,
        )

    for step in range(n_ctx):
        rows = slice(step * chunk, (step + 1) * chunk)
        part[rows, :] = dot_nt(mixed_ref[rows, :], proj_ref[:, 3 * columns :]).astype(BF16)
        exchange(step).start()
    for step in range(n_ctx):
        rows = slice(step * chunk, (step + 1) * chunk)
        exchange(step).wait_recv()
        branch = part[rows, :].astype(F32) + partner_part[rows, :].astype(F32)
        first_in_ref[rows, :] = x_ref[rows, :].astype(F32) + (branch + output_bias)

    for step in range(n_ctx):
        exchange(step).wait_send()
    for pair in range(pairs):
        for hop in range(1, n_ctx):
            moved(pair, hop).wait_send()
            sent_back(pair, hop).wait_send()
    if gathers:
        for copy in gather_copies:
            copy.wait_send()
        for copy in feed_copies:
            copy.wait_send()
        own[4].wait()
        own[5].wait()
        for step in range(1, n_dp):
            source = lax.rem(dp - step + n_dp, n_dp)
            rows = pl.ds(pl.multiple_of(source * shard, 16), shard)
            remote(
                outer_full_ref.at[rows],
                outer_full_ref.at[rows],
                feed_send.at[step],
                feed_recv.at[source],
                "dp",
                source,
            ).wait_recv()
            for hop in range(1, n_ctx):
                other = lax.rem(ctx - hop + n_ctx, n_ctx)
                remote(
                    strip(source, other),
                    strip(source, other),
                    inner_forward.at[step, hop],
                    inner_recv.at[other, source],
                    "context",
                    other,
                ).wait_recv()


def forward_attention(x, weights, cols, rows, biases, gathers):
    n_dp, n_ctx = lax.axis_size("dp"), lax.axis_size("context")
    slab, width = x.shape
    columns = weights[0].shape[1]
    hidden = weights[4].shape[1]
    pairs = columns // PAIR
    groups, share, chunk = slab // CLUSTER, CLUSTER // n_ctx, slab // n_ctx
    vmem = pl.BlockSpec(memory_space=pltpu.VMEM)
    hbm = pl.BlockSpec(memory_space=pl.ANY)
    dma = pltpu.SemaphoreType.DMA
    shapes = (
        jax.ShapeDtypeStruct((slab, width), F32),
        jax.ShapeDtypeStruct((slab, columns), BF16),
        jax.ShapeDtypeStruct((pairs, groups, CLUSTER, 3 * PAIR), BF16),
        jax.ShapeDtypeStruct((width, 4 * columns), BF16),
        jax.ShapeDtypeStruct((width, hidden), BF16),
        jax.ShapeDtypeStruct((width, hidden), BF16),
    )
    weight_spec = hbm if gathers else vmem
    return pl.pallas_call(
        functools.partial(forward_kernel, (n_dp, n_ctx, pairs, gathers)),
        out_shape=shapes,
        in_specs=[vmem] + [weight_spec] * 4 + [hbm] * 2 + [vmem] * 5,
        out_specs=(vmem, vmem, vmem, vmem, hbm, hbm),
        scratch_shapes=[
            pltpu.VMEM((pairs, slab, 3 * PAIR), BF16),
            pltpu.VMEM((pairs, n_ctx, groups, share, 3 * PAIR), BF16),
            pltpu.VMEM((pairs, groups, CLUSTER, PAIR), BF16),
            pltpu.VMEM((pairs, n_ctx, groups, share, PAIR), BF16),
            pltpu.VMEM((slab, width), BF16),
            pltpu.VMEM((slab, width), BF16),
            dma((6,)),
            dma((n_dp,)),
            dma((n_dp, n_ctx)),
            dma((4, n_dp)),
            dma((n_dp,)),
            dma((n_dp,)),
            dma((n_dp,)),
            dma((n_dp, n_ctx)),
            dma((n_ctx, n_dp)),
            dma((pairs, n_ctx)),
            dma((pairs, n_ctx)),
            dma((pairs, n_ctx)),
            dma((pairs, n_ctx)),
            dma((n_ctx,)),
            dma((n_ctx,)),
        ],
        compiler_params=pltpu.CompilerParams(collective_id=0, has_side_effects=True),
        name="forward_attention",
    )(x, *weights, cols, rows, *biases)


def store_chunk(ref, index, values):
    if len(ref.shape) == 3:
        ref[index] = values
        return
    n_ctx, n_dp, tile = ref.shape[1:4]
    for owner in range(n_dp):
        for place in range(n_ctx):
            row = (owner * n_ctx + place) * tile
            ref[index, place, owner] = values[row : row + tile]


def chunk_shape(count, width, columns, split):
    n_dp, n_ctx = lax.axis_size("dp"), lax.axis_size("context")
    if split:
        return (count, n_ctx, n_dp, width // (n_dp * n_ctx), columns)
    return (count, width, columns)


def sublane_sums(values):
    rows, width = values.shape
    return jnp.sum(values.reshape(rows // 8, 8, width), axis=0)


def feed_kernel(
    blocks,
    first_in_ref,
    cotangent_ref,
    inner_ref,
    outer_ref,
    inner_bias_ref,
    outer_bias_ref,
    first_gain_ref,
    first_shift_ref,
    second_gain_ref,
    second_shift_ref,
    activations_ref,
    summed_ref,
    branch_ref,
    inner_grad_ref,
    outer_grad_ref,
    sums_ref,
    low,
    first,
    act,
    slope,
    feed,
    part,
    partner_part,
    sums,
    pair_send,
    pair_recv,
):
    slab, width = first_in_ref.shape
    hidden = inner_ref.shape[1]
    chunk = slab // blocks
    core = lax.axis_index("tensor")
    meet(("tensor",))
    inner_bias, outer_bias = row_of(inner_bias_ref), row_of(outer_bias_ref)
    first_gain, first_shift = row_of(first_gain_ref), row_of(first_shift_ref)
    second_gain, second_shift = row_of(second_gain_ref), row_of(second_shift_ref)
    sums[...] = jnp.zeros_like(sums)

    def rows_of(step):
        return pl.ds(pl.multiple_of(step * chunk, chunk), chunk)

    def exchange(stage, step):
        return remote(
            part.at[stage, rows_of(step)],
            partner_part.at[stage, rows_of(step)],
            pair_send.at[stage, step],
            pair_recv.at[stage, step],
            "tensor",
            1 - core,
        )

    def expand(step, carry):
        rows = rows_of(step)
        normed, _ = normalize(first_in_ref[rows, :])
        values = normed * first_gain + first_shift
        first[rows, :] = values
        low[rows, :] = values.astype(BF16)
        inner = dot(low[rows, :], inner_ref[...]) + inner_bias
        cdf = 0.5 * (1.0 + lax.erf(inner * 0.7071067811865476))
        act[rows, :] = (inner * cdf).astype(BF16)
        slope[rows, :] = (
            cdf + inner * jnp.exp(-0.5 * inner * inner) * 0.3989422804014327
        ).astype(BF16)
        part[0, rows, :] = dot_nt(act[rows, :], outer_ref[...]).astype(BF16)
        exchange(0, step).start()
        return carry

    lax.fori_loop(0, blocks, expand, 0)

    def turn(step, carry):
        rows = rows_of(step)
        exchange(0, step).wait_recv()
        out = part[0, rows, :].astype(F32) + partner_part[0, rows, :].astype(F32)
        normed, root = normalize(first[rows, :] + (out + outer_bias))
        activations_ref[rows, :] = (
            normed * second_gain + second_shift
        ).astype(BF16)
        upstream = cotangent_ref[rows, :].astype(F32)
        grad = norm_backward(upstream, normed, root, second_gain)
        first[rows, :] = grad
        rounded = grad.astype(BF16)
        feed[rows, :] = rounded
        sums[2] += sublane_sums(rounded.astype(F32))
        sums[5] += sublane_sums(upstream * normed)
        sums[6] += sublane_sums(upstream)
        inner_grad = dot(rounded, outer_ref[...]) * slope[rows, :].astype(F32)
        slope[rows, :] = inner_grad.astype(BF16)
        inner_sums = sublane_sums(slope[rows, :].astype(F32))
        sums[0] += inner_sums[:, :width]
        sums[1] += inner_sums[:, width:]
        part[1, rows, :] = dot_nt(slope[rows, :], inner_ref[...]).astype(BF16)
        exchange(1, step).start()
        return carry

    lax.fori_loop(0, blocks, turn, 0)

    strip = hidden // blocks

    def weigh(step, carry):
        lanes = pl.ds(pl.multiple_of(step * strip, strip), strip)
        store_chunk(outer_grad_ref, step, dot_tn(feed[...], act[:, lanes]).astype(BF16))
        store_chunk(inner_grad_ref, step, dot_tn(low[...], slope[:, lanes]).astype(BF16))
        return carry

    lax.fori_loop(0, blocks, weigh, 0)

    def close(step, carry):
        rows = rows_of(step)
        exchange(1, step).wait_recv()
        back = part[1, rows, :].astype(F32) + partner_part[1, rows, :].astype(F32)
        grad = first[rows, :] + back
        normed, root = normalize(first_in_ref[rows, :])
        sums[3] += sublane_sums(grad * normed)
        sums[4] += sublane_sums(grad)
        summed = norm_backward(grad, normed, root, first_gain)
        summed_ref[rows, :] = summed
        rounded = summed.astype(BF16)
        branch_ref[rows, :] = rounded
        sums[7] += sublane_sums(rounded.astype(F32))
        return carry

    lax.fori_loop(0, blocks, close, 0)
    sums_ref[...] = jnp.sum(sums[...], axis=1)

    def finish(step, carry):
        exchange(0, step).wait_send()
        exchange(1, step).wait_send()
        return carry

    lax.fori_loop(0, blocks, finish, 0)


def feed_forward(first_in, cotangent, inner, outer, vectors, split):
    slab, width = first_in.shape
    hidden = inner.shape[1]
    blocks = lax.axis_size("context")
    vmem = pl.BlockSpec(memory_space=pltpu.VMEM)
    dma = pltpu.SemaphoreType.DMA
    return pl.pallas_call(
        functools.partial(feed_kernel, blocks),
        out_shape=(
            jax.ShapeDtypeStruct((slab, width), BF16),
            jax.ShapeDtypeStruct((slab, width), F32),
            jax.ShapeDtypeStruct((slab, width), BF16),
            jax.ShapeDtypeStruct(chunk_shape(blocks, width, hidden // blocks, split), BF16),
            jax.ShapeDtypeStruct(chunk_shape(blocks, width, hidden // blocks, split), BF16),
            jax.ShapeDtypeStruct((8, width), F32),
        ),
        in_specs=[vmem] * (4 + len(vectors)),
        out_specs=[vmem] * 6,
        scratch_shapes=[
            pltpu.VMEM((slab, width), BF16),
            pltpu.VMEM((slab, width), F32),
            pltpu.VMEM((slab, hidden), BF16),
            pltpu.VMEM((slab, hidden), BF16),
            pltpu.VMEM((slab, width), BF16),
            pltpu.VMEM((2, slab, width), BF16),
            pltpu.VMEM((2, slab, width), BF16),
            pltpu.VMEM((8, 8, width), F32),
            dma((2, blocks)),
            dma((2, blocks)),
        ],
        compiler_params=pltpu.CompilerParams(collective_id=1, has_side_effects=True),
        name="feed_forward",
    )(first_in, cotangent, inner, outer, *vectors)


def backward_kernel(
    sizes,
    x_ref,
    branch_ref,
    summed_ref,
    mixed_ref,
    got_ref,
    proj_ref,
    cols_ref,
    rows_ref,
    inner_part_ref,
    outer_part_ref,
    sums_ref,
    input_grad_ref,
    final_ref,
    totals_ref,
    proj_part_ref,
    upstream,
    sending,
    landed,
    answer,
    returned,
    restored,
    collected,
    pieces,
    gathered,
    part,
    partner_part,
    sums,
    sums_ctx,
    sums_dp,
    move_send,
    move_recv,
    back_send,
    back_recv,
    first_send,
    first_recv,
    second_send,
    second_recv,
    third_send,
    third_recv,
    sums_send,
    sums_recv,
    pair_send,
    pair_recv,
):
    n_dp, n_ctx, pairs, reduces = sizes
    slab, width = x_ref.shape
    columns = pairs * PAIR
    dp, ctx, core = lax.axis_index("dp"), lax.axis_index("context"), lax.axis_index("tensor")
    chunk = slab // n_ctx
    groups = slab // CLUSTER
    share = CLUSTER // n_ctx
    shard = width // n_dp
    meet(("dp", "context", "tensor") if reduces else ("context", "tensor"))

    def rows_of(step):
        return pl.ds(pl.multiple_of(step * chunk, chunk), chunk)

    strips = n_ctx
    half = strips // 2
    groups_of = [(proj_part_ref, number, 1, number, "context") for number in range(1 + pairs)]
    inner_near, inner_far, outer_far = range(1 + pairs, 4 + pairs)
    groups_of.append((inner_part_ref, 0, half, 1 + pairs, "context"))
    groups_of.append((inner_part_ref, half, strips - half, 1 + pairs + half, "dp"))
    groups_of.append((outer_part_ref, 0, strips, 1 + pairs + strips, "dp"))
    places = {"context": (n_ctx, ctx, "dp"), "dp": (n_dp, dp, "context")}

    def first(group, hop):
        source, start, count, chunk, axis = groups_of[group]
        size, own, _ = places[axis]
        target = lax.rem(own + hop, size)
        if axis == "context":
            sent = source.at[start : start + count, target]
        else:
            sent = source.at[start : start + count, :, target]
        landing = collected.at[hop, chunk : chunk + count]
        if hop == 0:
            return pltpu.make_async_copy(sent, landing, first_recv.at[group, 0])
        return remote(
            sent, landing, first_send.at[group, hop], first_recv.at[group, hop], axis, target
        )

    def second(group, hop):
        _, _, count, chunk, axis = groups_of[group]
        other = places[axis][2]
        size, own, _ = places[other]
        target = lax.rem(own + hop, size)
        return remote(
            pieces.at[chunk : chunk + count, target],
            gathered.at[hop, chunk : chunk + count],
            second_send.at[group, hop],
            second_recv.at[group, hop],
            other,
            target,
        )

    def third(group, hop, mine):
        _, _, count, chunk, _ = groups_of[group]
        owner = ctx if mine else lax.rem(ctx - hop + n_ctx, n_ctx)
        block = final_ref.at[chunk : chunk + count, owner]
        return remote(
            block,
            block,
            third_send.at[group, hop],
            third_recv.at[group, hop],
            "context",
            lax.rem(ctx + hop, n_ctx),
        )

    def first_size(group):
        return places[groups_of[group][4]][0]

    def second_size(group):
        return places[places[groups_of[group][4]][2]][0]

    def start_first(group):
        for hop in (*range(1, first_size(group)), 0):
            first(group, hop).start()

    def sum_first(group):
        _, _, count, chunk, _ = groups_of[group]
        first(group, 0).wait()
        for hop in range(1, first_size(group)):
            first(group, hop).wait_recv()

        def add(step, carry):
            total = collected[0, chunk + step].astype(F32)
            for hop in range(1, first_size(group)):
                total = total + collected[hop, chunk + step].astype(F32)
            pieces[chunk + step] = total.astype(BF16)
            return carry

        lax.fori_loop(0, count, add, 0)
        for hop in range(1, second_size(group)):
            second(group, hop).start()

    def sum_second(group):
        _, _, count, chunk, axis = groups_of[group]
        own = places[places[axis][2]][1]
        for hop in range(1, second_size(group)):
            second(group, hop).wait_recv()
        for number in range(chunk, chunk + count):
            total = pieces[number, own].astype(F32)
            for hop in range(1, second_size(group)):
                total = total + gathered[hop, number].astype(F32)
            final_ref[number, ctx] = total.astype(BF16)
        for hop in range(1, n_ctx):
            third(group, hop, True).start()

    if reduces:
        start_first(outer_far)
        start_first(inner_far)

    def project(step, carry):
        rows = rows_of(step)
        upstream[rows, :] = dot(branch_ref[rows, :], proj_ref[:, 3 * columns :]).astype(BF16)
        return carry

    lax.fori_loop(0, n_ctx, project, 0)

    own_share = pl.ds(pl.multiple_of(ctx * share, share), share)

    def moved(pair, hop):
        target = lax.rem(ctx + hop, n_ctx)
        source = sending.at[pair, target]
        landing = landed.at[pair, :, own_share, :]
        if hop == 0:
            return pltpu.make_async_copy(source, landing, move_recv.at[pair, 0])
        return remote(
            source, landing, move_send.at[pair, hop], move_recv.at[pair, hop], "context", target
        )

    for pair in range(pairs):
        for hop in (*range(1, n_ctx), 0):
            target = lax.rem(ctx + hop, n_ctx)
            rows = rows_of(target)
            positions = lax.broadcasted_iota(jnp.int32, (chunk, slab), 1)
            values = upstream[:, pair * PAIR : (pair + 1) * PAIR]
            even = dot(one_hot(cols_ref[rows, 2 * pair : 2 * pair + 1], positions), values)
            odd = dot(one_hot(cols_ref[rows, 2 * pair + 1 : 2 * pair + 2], positions), values)
            picked = jnp.where(low_lanes(even.shape), even, odd).astype(BF16)
            sending[pair, target] = picked.reshape(groups, share, PAIR)
            moved(pair, hop).start()

    if reduces:
        start_first(inner_near)
    store_chunk(proj_part_ref, 0, dot_tn(branch_ref[...], mixed_ref[...]).astype(BF16))
    if reduces:
        start_first(0)

    def sent_back(pair, hop):
        target = lax.rem(ctx - hop + n_ctx, n_ctx)
        rows = pl.ds(pl.multiple_of(target * share, share), share)
        source = answer.at[pair, :, rows, :]
        landing = returned.at[pair, ctx]
        if hop == 0:
            return pltpu.make_async_copy(source, landing, back_recv.at[pair, 0])
        return remote(
            source, landing, back_send.at[pair, hop], back_recv.at[pair, hop], "context", target
        )

    for pair in range(pairs):
        for hop in range(n_ctx):
            copy = moved(pair, hop)
            if hop == 0:
                copy.wait()
            else:
                copy.wait_recv()

        def attend(group, carry):
            query2 = stack_pair(got_ref[pair, group, :, 0:PAIR])
            key = got_ref[pair, group, :, PAIR : 2 * PAIR]
            value = got_ref[pair, group, :, 2 * PAIR : 3 * PAIR]
            grad2 = stack_pair(landed[pair, group])
            masks = pair_mask(cols_ref, rows_ref, pair, group, 2 * pairs)
            raw = dot_nt(query2, key) * HEAD_DIM ** (-0.5)
            scores = jnp.concatenate(
                [
                    jnp.where(mask, raw[i * CLUSTER : (i + 1) * CLUSTER], masked_score)
                    for i, mask in enumerate(masks)
                ],
                axis=0,
            )
            exponent = jnp.exp(scores - jnp.max(scores, axis=1, keepdims=True))
            probs = exponent / jnp.sum(exponent, axis=1, keepdims=True)
            prob_grad = dot_nt(grad2, value)
            inner = jnp.sum(probs * prob_grad, axis=1, keepdims=True)
            score_grad = (probs * (prob_grad - inner) * HEAD_DIM ** (-0.5)).astype(BF16)
            value_grad = dot_tn(probs.astype(BF16), grad2)
            query_grad = fold_pair(dot(score_grad, key))
            key_grad = dot_tn(score_grad, query2)
            low = low_lanes((CLUSTER, PAIR))
            first = jnp.where(low, query_grad, pltpu.roll(key_grad, HEAD_DIM, 1))
            second = jnp.where(low, pltpu.roll(query_grad, HEAD_DIM, 1), key_grad)
            answer[pair, group, :, 0:PAIR] = first.astype(BF16)
            answer[pair, group, :, PAIR : 2 * PAIR] = second.astype(BF16)
            answer[pair, group, :, 2 * PAIR : 3 * PAIR] = value_grad.astype(BF16)
            return carry

        lax.fori_loop(0, groups, attend, 0, unroll=2)
        for hop in (*range(1, n_ctx), 0):
            sent_back(pair, hop).start()

    if reduces:
        sum_first(0)
    for pair in range(pairs):
        for hop in range(n_ctx):
            copy = sent_back(pair, hop)
            if hop == 0:
                copy.wait()
            else:
                copy.wait_recv()

        def restore(step, carry):
            rows = rows_of(step)
            positions = lax.broadcasted_iota(jnp.int32, (chunk, slab), 0) + step * chunk
            values = returned[pair].reshape(slab, 3 * PAIR)
            shared = values[:, 2 * PAIR :]
            even = dot(
                one_hot(rows_ref[2 * pair : 2 * pair + 1, :], positions),
                jnp.concatenate((values[:, :PAIR], shared), axis=1),
            )
            odd = dot(
                one_hot(rows_ref[2 * pair + 1 : 2 * pair + 2, :], positions), values[:, PAIR:]
            )
            low = low_lanes((chunk, PAIR))
            first, second = even[:, :PAIR], odd[:, :PAIR]
            query = jnp.where(low, first, pltpu.roll(second, HEAD_DIM, 1))
            key = jnp.where(low, pltpu.roll(first, HEAD_DIM, 1), second)
            value = jnp.where(low, even[:, PAIR:], odd[:, PAIR:])
            for number, piece in enumerate((query, key, value)):
                lanes = slice(number * columns + pair * PAIR, number * columns + (pair + 1) * PAIR)
                restored[rows, lanes] = piece.astype(BF16)
            return carry

        lax.fori_loop(0, n_ctx, restore, 0)
        grads = jnp.concatenate(
            [
                restored[:, number * columns + pair * PAIR : number * columns + (pair + 1) * PAIR]
                for number in range(3)
            ],
            axis=1,
        )
        store_chunk(proj_part_ref, 1 + pair, dot_tn(x_ref[...], grads).astype(BF16))
        if reduces:
            start_first(1 + pair)

    def exchange(step):
        return remote(
            part.at[rows_of(step)],
            partner_part.at[rows_of(step)],
            pair_send.at[step],
            pair_recv.at[step],
            "tensor",
            1 - core,
        )

    def give(step, carry):
        rows = rows_of(step)
        part[rows, :] = dot_nt(restored[rows, :], proj_ref[:, : 3 * columns]).astype(BF16)
        exchange(step).start()
        return carry

    lax.fori_loop(0, n_ctx, give, 0)

    sums[0:8, :] = sums_ref[...]
    sums[8:16, :] = jnp.zeros((8, width), F32)
    for place, number in enumerate((0, 2)):
        values = restored[:, number * columns : (number + 1) * columns].astype(F32)
        sums[8:9, place * columns : (place + 1) * columns] = jnp.sum(values, axis=0, keepdims=True)

    def sums_out(level, step):
        axis, size, own = (("context", n_ctx, ctx), ("dp", n_dp, dp))[level]
        landing = (sums_ctx, sums_dp)[level]
        return remote(
            sums.at[level * 16 : level * 16 + 16],
            landing.at[own],
            sums_send.at[level, step],
            sums_recv.at[level, step],
            axis,
            lax.rem(own + step, size),
        )

    if reduces:
        for step in range(1, n_ctx):
            sums_out(0, step).start()
        sums_ctx[ctx] = sums[0:16, :]

    def take(step, carry):
        rows = rows_of(step)
        exchange(step).wait_recv()
        back = part[rows, :].astype(F32) + partner_part[rows, :].astype(F32)
        input_grad_ref[rows, :] = (summed_ref[rows, :] + back).astype(BF16)
        return carry

    if reduces:
        sum_first(outer_far)
        sum_first(inner_near)
    lax.fori_loop(0, n_ctx, take, 0)

    if reduces:
        for step in range(1, n_ctx):
            sums_out(0, step).wait_recv()
        sums[16:32, :] = jnp.sum(sums_ctx[...], axis=0)
        for step in range(1, n_dp):
            sums_out(1, step).start()
        sums_dp[dp] = sums[16:32, :]
        for pair in range(pairs - 1):
            sum_first(1 + pair)
        sum_first(inner_far)
        sum_first(pairs)
        sum_second(outer_far)
        sum_second(0)
        sum_second(inner_near)
        for step in range(1, n_dp):
            sums_out(1, step).wait_recv()
        totals_ref[...] = jnp.sum(sums_dp[...], axis=0)
        for pair in range(pairs - 1):
            sum_second(1 + pair)
        sum_second(inner_far)
        sum_second(pairs)
        for group in range(4 + pairs):
            for hop in range(1, n_ctx):
                third(group, hop, False).wait_recv()
            for hop in range(1, n_ctx):
                third(group, hop, True).wait_send()
            for hop in range(1, first_size(group)):
                first(group, hop).wait_send()
            for hop in range(1, second_size(group)):
                second(group, hop).wait_send()
        for level, size in enumerate((n_ctx, n_dp)):
            for step in range(1, size):
                sums_out(level, step).wait_send()
    else:
        totals_ref[...] = sums[0:16, :]
    for step in range(n_ctx):
        exchange(step).wait_send()
    for pair in range(pairs):
        for hop in range(1, n_ctx):
            moved(pair, hop).wait_send()
            sent_back(pair, hop).wait_send()


def backward_attention(
    x, branch, summed, mixed, got, proj, cols, rows, inner_part, outer_part, sums, reduces
):
    n_dp, n_ctx = lax.axis_size("dp"), lax.axis_size("context")
    slab, width = x.shape
    columns = mixed.shape[1]
    pairs = columns // PAIR
    groups, share = slab // CLUSTER, CLUSTER // n_ctx
    shard = width // n_dp
    vmem = pl.BlockSpec(memory_space=pltpu.VMEM)
    hbm = pl.BlockSpec(memory_space=pl.ANY)
    dma = pltpu.SemaphoreType.DMA
    chunks, steps = (1 + pairs + 2 * n_ctx, n_dp) if reduces else (1, 1)
    tile = shard // n_ctx if reduces else 16
    total = 4 + pairs
    hops = max(n_ctx, steps)
    return pl.pallas_call(
        functools.partial(backward_kernel, (n_dp, n_ctx, pairs, reduces)),
        out_shape=(
            jax.ShapeDtypeStruct((slab, width), BF16),
            jax.ShapeDtypeStruct((chunks, n_ctx, tile, columns), BF16),
            jax.ShapeDtypeStruct((16, width), F32),
            jax.ShapeDtypeStruct(chunk_shape(1 + pairs, width, columns, reduces), BF16),
        ),
        in_specs=[vmem] * 8 + [hbm] * 2 + [vmem],
        out_specs=[vmem] * 4,
        scratch_shapes=[
            pltpu.VMEM((slab, columns), BF16),
            pltpu.VMEM((pairs, n_ctx, groups, share, PAIR), BF16),
            pltpu.VMEM((pairs, groups, CLUSTER, PAIR), BF16),
            pltpu.VMEM((pairs, groups, CLUSTER, 3 * PAIR), BF16),
            pltpu.VMEM((pairs, n_ctx, groups, share, 3 * PAIR), BF16),
            pltpu.VMEM((slab, 3 * columns), BF16),
            pltpu.VMEM((hops, chunks, n_ctx, tile, columns), BF16),
            pltpu.VMEM((chunks, n_ctx, tile, columns), BF16),
            pltpu.VMEM((hops, chunks, tile, columns), BF16),
            pltpu.VMEM((slab, width), BF16),
            pltpu.VMEM((slab, width), BF16),
            pltpu.VMEM((32, width), F32),
            pltpu.VMEM((n_ctx, 16, width), F32),
            pltpu.VMEM((steps, 16, width), F32),
            dma((pairs, n_ctx)),
            dma((pairs, n_ctx)),
            dma((pairs, n_ctx)),
            dma((pairs, n_ctx)),
            dma((total, hops)),
            dma((total, hops)),
            dma((total, hops)),
            dma((total, hops)),
            dma((total, hops)),
            dma((total, hops)),
            dma((2, hops)),
            dma((2, hops)),
            dma((n_ctx,)),
            dma((n_ctx,)),
        ],
        compiler_params=pltpu.CompilerParams(collective_id=2, has_side_effects=True),
        name="backward_attention",
    )(x, branch, summed, mixed, got, proj, cols, rows, inner_part, outer_part, sums)


def results_kernel(
    activations_in,
    input_grad_in,
    final_ref,
    totals_ref,
    activations_ref,
    input_grad_ref,
    query_ref,
    key_ref,
    value_ref,
    output_ref,
    inner_ref,
    outer_ref,
    query_bias_ref,
    value_bias_ref,
    output_bias_ref,
    inner_bias_ref,
    outer_bias_ref,
    first_gain_ref,
    first_shift_ref,
    second_gain_ref,
    second_shift_ref,
):
    chunks, blocks, tile, columns = final_ref.shape
    width = totals_ref.shape[1]
    pairs = columns // PAIR
    strips = (chunks - 1 - pairs) // 2
    activations_ref[...] = activations_in[...]
    input_grad_ref[...] = input_grad_in[...]
    for block in range(blocks):
        rows = slice(block * tile, (block + 1) * tile)
        output_ref[rows, :] = final_ref[0, block].astype(F32)
        for pair in range(pairs):
            lanes = slice(pair * PAIR, (pair + 1) * PAIR)
            for number, ref in enumerate((query_ref, key_ref, value_ref)):
                part = final_ref[1 + pair, block, :, number * PAIR : (number + 1) * PAIR]
                ref[rows, lanes] = part.astype(F32)
        for number, ref in enumerate((inner_ref, outer_ref)):
            for strip in range(strips):
                lanes = slice(strip * columns, (strip + 1) * columns)
                chunk = 1 + pairs + number * strips + strip
                ref[rows, lanes] = final_ref[chunk, block].astype(F32)
    query_bias_ref[...] = totals_ref[8, :columns]
    value_bias_ref[...] = totals_ref[8, columns:]
    output_bias_ref[...] = totals_ref[7, :]
    inner_bias_ref[:width] = totals_ref[0, :]
    inner_bias_ref[width:] = totals_ref[1, :]
    rest = (outer_bias_ref, first_gain_ref, first_shift_ref, second_gain_ref, second_shift_ref)
    for number, ref in enumerate(rest):
        ref[...] = totals_ref[2 + number, :]


def write_results(activations, input_grad, final, totals):
    chunks, blocks, tile, columns = final.shape
    slab, width = activations.shape
    shard = blocks * tile
    hidden = (chunks - 1 - columns // PAIR) // 2 * columns
    shapes = (
        [(shard, columns)] * 4
        + [(shard, hidden)] * 2
        + [(columns,)] * 2
        + [(width,), (hidden,)]
        + [(width,)] * 5
    )
    vmem = pl.BlockSpec(memory_space=pltpu.VMEM)
    results = pl.pallas_call(
        results_kernel,
        out_shape=[jax.ShapeDtypeStruct((slab, width), BF16)] * 2
        + [jax.ShapeDtypeStruct(shape, F32) for shape in shapes],
        in_specs=[vmem] * 4,
        out_specs=[vmem] * 17,
        name="write_results",
    )(activations, input_grad, final, totals)
    activations, input_grad, query, key, value, output, inner, outer = results[:8]
    return (
        activations[None],
        input_grad[None],
        query,
        key,
        value,
        output.T,
        inner,
        outer.T,
        *results[8:],
    )


def slot_tables(cluster_order, prefix_length, own, n_ctx):
    heads, length = cluster_order.shape[1:]
    slab = length // n_ctx
    order = cluster_order.reshape(heads, n_ctx, slab // CLUSTER, n_ctx, CLUSTER // n_ctx)
    rows = lax.dynamic_index_in_dim(order, own, axis=3, keepdims=False).reshape(heads, slab)
    rows = rows - own * slab
    places = lax.dynamic_slice_in_dim(cluster_order[0], own * slab, slab, axis=1)
    gap = jnp.zeros((8 - heads % 8, slab), jnp.int32)
    limits = jnp.maximum(places, prefix_length[0] - 1)
    along = jnp.concatenate((rows, gap, places, gap), axis=0)
    down = jnp.concatenate((rows, gap, limits, gap), axis=0).T
    return down, along


def shards(
    tokens,
    prefix_length,
    cluster_order,
    query_weight,
    key_weight,
    value_weight,
    output_weight,
    inner_weight,
    outer_weight,
    query_bias,
    value_bias,
    output_bias,
    inner_bias,
    outer_bias,
    first_gain,
    first_shift,
    second_gain,
    second_shift,
    cotangent,
):
    n_ctx = lax.axis_size("context")
    own = lax.axis_index("context")
    x = tokens[0]
    shard, columns = query_weight.shape
    aligned = n_ctx == lax.axis_size("dp") and shard % (16 * n_ctx) == 0
    weights = (query_weight, key_weight, value_weight, output_weight.T, inner_weight, outer_weight.T)
    if not aligned:
        weights = tuple(lax.all_gather(w, "dp", axis=0, tiled=True) for w in weights)
    cols, rows = slot_tables(cluster_order, prefix_length, own, n_ctx)
    biases = (query_bias, value_bias, output_bias)
    vectors = (inner_bias, outer_bias, first_gain, first_shift, second_gain, second_shift)
    first_in, mixed, got, proj, inner_full, outer_full = forward_attention(
        x, weights, cols, rows, biases, aligned
    )
    if not aligned:
        inner_full, outer_full = weights[4:]
    activations, summed, branch, inner_part, outer_part, sums = feed_forward(
        first_in, cotangent[0], inner_full, outer_full, vectors, aligned
    )
    input_grad, final, totals, proj_part = backward_attention(
        x, branch, summed, mixed, got, proj, cols, rows, inner_part, outer_part, sums, aligned
    )
    if not aligned:
        parts = jnp.concatenate((proj_part, inner_part, outer_part), axis=0)
        piece = lax.psum_scatter(parts, "dp", scatter_dimension=1, tiled=True)
        final = lax.psum(piece, "context")[:, None]
        totals = lax.psum(totals, ("dp", "context"))
    return write_results(activations, input_grad, final, totals)


def solution(mesh):
    placed = (
        P("dp", "context", None),
        P("dp"),
        P("dp", "tensor", None),
        P("dp", "tensor"),
        P("dp", "tensor"),
        P("dp", "tensor"),
        P("tensor", "dp"),
        P("dp", "tensor"),
        P("tensor", "dp"),
        P("tensor"),
        P("tensor"),
        P(),
        P("tensor"),
        P(),
        P(),
        P(),
        P(),
        P(),
        P("dp", "context", None),
    )
    return jax.shard_map(
        shards,
        mesh=mesh,
        in_specs=placed,
        out_specs=(
            P("dp", "context", None),
            P("dp", "context", None),
            P("dp", "tensor"),
            P("dp", "tensor"),
            P("dp", "tensor"),
            P("tensor", "dp"),
            P("dp", "tensor"),
            P("tensor", "dp"),
            P("tensor"),
            P("tensor"),
            P(),
            P("tensor"),
            P(),
            P(),
            P(),
            P(),
            P(),
        ),
        check_vma=False,
    )
```

```python
import functools

import jax
import jax.numpy as jnp
from jax import lax
from jax.experimental import pallas as pl
from jax.experimental.pallas import tpu as pltpu
from jax.sharding import PartitionSpec as P

HEAD_DIM = 64
CLUSTER = 128


norm_epsilon = 1e-12
masked_score = -1e30


def normalize(values):
    center = values - jnp.mean(values, axis=-1, keepdims=True)
    inverse_root = lax.rsqrt(jnp.mean(center * center, axis=-1, keepdims=True) + norm_epsilon)
    return (center * inverse_root, inverse_root)


def norm_backward(upstream, normed, inverse_root, gain):
    scaled = upstream * gain
    centered = scaled - jnp.mean(scaled, axis=-1, keepdims=True)
    return inverse_root * (centered - normed * jnp.mean(scaled * normed, axis=-1, keepdims=True))


MESH = pl.DeviceIdType.MESH
BF16 = jnp.bfloat16
F32 = jnp.float32
PAIR = 2 * HEAD_DIM


def dot(a, b):
    return lax.dot_general(a, b, (((1,), (0,)), ((), ())), preferred_element_type=F32)


def dot_nt(a, b):
    return lax.dot_general(a, b, (((1,), (1,)), ((), ())), preferred_element_type=F32)


def dot_tn(a, b):
    return lax.dot_general(a, b, (((0,), (0,)), ((), ())), preferred_element_type=F32)


def remote(src, dst, send_sem, recv_sem, axis, index):
    return pltpu.make_async_remote_copy(
        src_ref=src,
        dst_ref=dst,
        send_sem=send_sem,
        recv_sem=recv_sem,
        device_id={axis: index},
        device_id_type=MESH,
    )


def partner(own, hop, size):
    place, bit = own, 1
    while bit < size:
        if hop & bit:
            place = place + bit * (1 - 2 * lax.rem(lax.div(own, bit), 2))
        bit *= 2
    return place


def peer(axis, own, hop, size):
    return partner(own, hop, size) if axis == "context" else lax.rem(own + hop, size)


def meet(axes):
    barrier = pltpu.get_barrier_semaphore()
    count = 0
    for axis in axes:
        size, own = lax.axis_size(axis), lax.axis_index(axis)
        for step in range(1, size):
            pl.semaphore_signal(
                barrier,
                inc=1,
                device_id={axis: lax.rem(own + step, size)},
                device_id_type=MESH,
            )
            count += 1
    pl.semaphore_wait(barrier, count)


def row_of(ref):
    return ref[...].reshape(1, ref.shape[0])


def low_lanes(shape):
    return lax.broadcasted_iota(jnp.int32, shape, 1) < HEAD_DIM


def one_hot(left, right):
    return jnp.where(left == right, 1.0, 0.0).astype(BF16)


def stack_pair(pair):
    low = low_lanes(pair.shape)
    zero = jnp.zeros_like(pair)
    return jnp.concatenate((jnp.where(low, pair, zero), jnp.where(low, zero, pair)), axis=0)


def fold_pair(stacked):
    rows = stacked.shape[0] // 2
    top, bottom = stacked[:rows], stacked[rows:]
    return jnp.where(low_lanes(top.shape), top, bottom)


def pair_scores(query2, key, mask2):
    raw = dot_nt(query2, key) * HEAD_DIM ** (-0.5)
    return jnp.where(mask2, raw, masked_score)


def pair_mask(cols_ref, rows_ref, pair, group, heads):
    row = pl.multiple_of(group * CLUSTER, CLUSTER)
    parts = []
    for head in (2 * pair, 2 * pair + 1):
        limit = cols_ref[pl.ds(row, CLUSTER), 8 + head : 9 + head]
        place = rows_ref[8 + head : 9 + head, pl.ds(row, CLUSTER)]
        parts.append(place <= limit)
    return parts


def forward_kernel(
    sizes,
    x_ref,
    query_ref,
    key_ref,
    value_ref,
    output_ref,
    inner_ref,
    outer_ref,
    cols_ref,
    rows_ref,
    query_bias_ref,
    value_bias_ref,
    output_bias_ref,
    first_in_ref,
    mixed_ref,
    got_ref,
    proj_ref,
    inner_full_ref,
    outer_full_ref,
    packed,
    sending,
    answer,
    returned,
    part,
    partner_part,
    own_sem,
    gather_send,
    forward_send,
    gather_recv,
    feed_send,
    feed_recv,
    inner_send,
    inner_forward,
    inner_recv,
    move_send,
    move_recv,
    back_send,
    back_recv,
    pair_send,
    pair_recv,
):
    n_dp, n_ctx, pairs, gathers = sizes
    slab, width = x_ref.shape
    columns = pairs * PAIR
    dp, ctx, core = lax.axis_index("dp"), lax.axis_index("context"), lax.axis_index("tensor")
    chunk = slab // n_ctx
    groups = slab // CLUSTER
    share = CLUSTER // n_ctx
    shard = width // n_dp
    meet(("dp", "context", "tensor") if gathers else ("context", "tensor"))

    own_rows = pl.ds(pl.multiple_of(dp * shard, 16) if gathers else 0, shard)
    feed_copies = []
    if gathers:
        own = []
        for number, source in enumerate((query_ref, key_ref, value_ref, output_ref)):
            own.append(
                pltpu.make_async_copy(
                    source,
                    proj_ref.at[own_rows, pl.ds(number * columns, columns)],
                    own_sem.at[number],
                )
            )
        own.append(pltpu.make_async_copy(inner_ref, inner_full_ref.at[own_rows], own_sem.at[4]))
        own.append(pltpu.make_async_copy(outer_ref, outer_full_ref.at[own_rows], own_sem.at[5]))
        for copy in own:
            copy.start()

        def block(rows_of, block_number):
            rows = pl.ds(pl.multiple_of(rows_of * shard, 16), shard)
            lanes = pl.ds(pl.multiple_of(block_number * columns, columns), columns)
            return proj_ref.at[rows, lanes]

        for copy in own[:4]:
            copy.wait()
        gather_copies = []
        for step in range(1, n_dp):
            copy = remote(
                block(dp, ctx),
                block(dp, ctx),
                gather_send.at[step],
                gather_recv.at[ctx, dp],
                "dp",
                lax.rem(dp + step, n_dp),
            )
            copy.start()
            gather_copies.append(copy)

        def strip(rows_of, block_number):
            rows = pl.ds(pl.multiple_of(rows_of * shard, 16), shard)
            lanes = pl.ds(pl.multiple_of(block_number * columns, columns), columns)
            return inner_full_ref.at[rows, lanes]

        own_lanes = pl.ds(pl.multiple_of(ctx * columns, columns), columns)
        for step in range(1, n_dp):
            copy = remote(
                inner_ref.at[:, own_lanes],
                strip(dp, ctx),
                inner_send.at[step],
                inner_recv.at[ctx, dp],
                "dp",
                lax.rem(dp + step, n_dp),
            )
            copy.start()
            feed_copies.append(copy)
        for step in range(1, n_dp):
            copy = remote(
                outer_ref,
                outer_full_ref.at[own_rows],
                feed_send.at[step],
                feed_recv.at[dp],
                "dp",
                lax.rem(dp + step, n_dp),
            )
            copy.start()
            feed_copies.append(copy)

        def forward_strip(step):
            source = lax.rem(dp - step + n_dp, n_dp)
            remote(
                strip(source, ctx),
                strip(source, ctx),
                inner_send.at[step],
                inner_recv.at[ctx, source],
                "dp",
                source,
            ).wait_recv()
            for hop in range(1, n_ctx):
                copy = remote(
                    strip(source, ctx),
                    strip(source, ctx),
                    inner_forward.at[step, hop],
                    inner_recv.at[ctx, source],
                    "context",
                    partner(ctx, hop, n_ctx),
                )
                copy.start()
                feed_copies.append(copy)

        for step in range(1, n_dp):
            source = lax.rem(dp - step + n_dp, n_dp)
            remote(
                block(source, ctx),
                block(source, ctx),
                gather_send.at[step],
                gather_recv.at[ctx, source],
                "dp",
                source,
            ).wait_recv()
            for hop in range(1, n_ctx):
                copy = remote(
                    block(source, ctx),
                    block(source, ctx),
                    forward_send.at[step, hop],
                    gather_recv.at[ctx, source],
                    "context",
                    partner(ctx, hop, n_ctx),
                )
                copy.start()
                gather_copies.append(copy)
        for hop in range(1, n_ctx):
            other = partner(ctx, hop, n_ctx)
            for step in range(1, n_dp):
                source = lax.rem(dp - step + n_dp, n_dp)
                remote(
                    block(source, other),
                    block(source, other),
                    forward_send.at[step, hop],
                    gather_recv.at[other, source],
                    "context",
                    other,
                ).wait_recv()
    else:
        for number, source in enumerate((query_ref, key_ref, value_ref, output_ref)):
            proj_ref[:, number * columns : (number + 1) * columns] = source[...]

    query_bias, value_bias = row_of(query_bias_ref), row_of(value_bias_ref)
    output_bias = row_of(output_bias_ref)

    def project(step, carry):
        rows = pl.ds(pl.multiple_of(step * chunk, chunk), chunk)
        values = dot(x_ref[rows, :], proj_ref[:, : 3 * columns])
        low = low_lanes((chunk, PAIR))
        for pair in range(pairs):
            lanes = slice(pair * PAIR, (pair + 1) * PAIR)
            query = values[:, lanes] + query_bias[:, lanes]
            key = values[:, columns + pair * PAIR : columns + (pair + 1) * PAIR]
            value = (
                values[:, 2 * columns + pair * PAIR : 2 * columns + (pair + 1) * PAIR]
                + value_bias[:, lanes]
            )
            first = jnp.where(low, query, pltpu.roll(key, HEAD_DIM, 1))
            second = jnp.where(low, pltpu.roll(query, HEAD_DIM, 1), key)
            packed[pair, rows, 0:PAIR] = first.astype(BF16)
            packed[pair, rows, PAIR : 2 * PAIR] = second.astype(BF16)
            packed[pair, rows, 2 * PAIR : 3 * PAIR] = value.astype(BF16)
        return carry

    if gathers:
        forward_strip(1)
    lax.fori_loop(0, n_ctx, project, 0)

    own_share = pl.ds(pl.multiple_of(ctx * share, share), share)

    def pick(pair, target):
        rows = pl.ds(pl.multiple_of(target * chunk, chunk), chunk)
        positions = lax.broadcasted_iota(jnp.int32, (chunk, slab), 1)
        tables = [
            one_hot(cols_ref[rows, head : head + 1], positions) for head in (2 * pair, 2 * pair + 1)
        ]
        shared = packed[pair, :, 2 * PAIR : 3 * PAIR]
        even = dot(tables[0], jnp.concatenate((packed[pair, :, 0:PAIR], shared), axis=1))
        odd = dot(tables[1], jnp.concatenate((packed[pair, :, PAIR : 2 * PAIR], shared), axis=1))
        low = low_lanes((chunk, PAIR))
        query = jnp.where(low, even[:, :PAIR], pltpu.roll(odd[:, :PAIR], HEAD_DIM, 1))
        key = jnp.where(low, pltpu.roll(even[:, :PAIR], HEAD_DIM, 1), odd[:, :PAIR])
        value = jnp.where(low, even[:, PAIR:], odd[:, PAIR:])
        for number, piece in enumerate((query, key, value)):
            sending[pair, target, :, :, number * PAIR : (number + 1) * PAIR] = piece.astype(
                BF16
            ).reshape(groups, share, PAIR)

    def moved(pair, hop):
        target = partner(ctx, hop, n_ctx)
        source = sending.at[pair, target]
        landing = got_ref.at[pair, :, own_share, :]
        if hop == 0:
            return pltpu.make_async_copy(source, landing, move_recv.at[pair, 0])
        return remote(
            source, landing, move_send.at[pair, hop], move_recv.at[pair, hop], "context", target
        )

    for pair in range(pairs):
        for hop in (*range(1, n_ctx), 0):
            pick(pair, partner(ctx, hop, n_ctx))
            moved(pair, hop).start()

    def sent_back(pair, hop):
        target = partner(ctx, hop, n_ctx)
        rows = pl.ds(pl.multiple_of(target * share, share), share)
        source = answer.at[pair, :, rows, :]
        landing = returned.at[pair, ctx]
        if hop == 0:
            return pltpu.make_async_copy(source, landing, back_recv.at[pair, 0])
        return remote(
            source, landing, back_send.at[pair, hop], back_recv.at[pair, hop], "context", target
        )

    for pair in range(pairs):
        for hop in range(n_ctx):
            copy = moved(pair, hop)
            if hop == 0:
                copy.wait()
            else:
                copy.wait_recv()

        def attend(group, carry):
            query2 = stack_pair(got_ref[pair, group, :, 0:PAIR])
            key = got_ref[pair, group, :, PAIR : 2 * PAIR]
            value = got_ref[pair, group, :, 2 * PAIR : 3 * PAIR]
            masks = pair_mask(cols_ref, rows_ref, pair, group, 2 * pairs)
            raw = dot_nt(query2, key) * HEAD_DIM ** (-0.5)
            scores = jnp.concatenate(
                [
                    jnp.where(mask, raw[i * CLUSTER : (i + 1) * CLUSTER], masked_score)
                    for i, mask in enumerate(masks)
                ],
                axis=0,
            )
            exponent = jnp.exp(scores - jnp.max(scores, axis=1, keepdims=True))
            total = jnp.sum(exponent, axis=1, keepdims=True)
            weights = (exponent / total).astype(BF16)
            answer[pair, group] = fold_pair(dot(weights, value)).astype(BF16)
            return carry

        lax.fori_loop(0, groups, attend, 0, unroll=2)
        for hop in (*range(1, n_ctx), 0):
            sent_back(pair, hop).start()
    if gathers:
        for step in range(2, n_dp):
            forward_strip(step)

    for pair in range(pairs):
        for hop in range(n_ctx):
            copy = sent_back(pair, hop)
            if hop == 0:
                copy.wait()
            else:
                copy.wait_recv()

        def restore(step, carry):
            rows = pl.ds(pl.multiple_of(step * chunk, chunk), chunk)
            positions = lax.broadcasted_iota(jnp.int32, (chunk, slab), 0) + step * chunk
            values = returned[pair].reshape(slab, PAIR)
            even = dot(one_hot(rows_ref[2 * pair : 2 * pair + 1, :], positions), values)
            odd = dot(one_hot(rows_ref[2 * pair + 1 : 2 * pair + 2, :], positions), values)
            mixed_ref[rows, pair * PAIR : (pair + 1) * PAIR] = jnp.where(
                low_lanes(even.shape), even, odd
            ).astype(BF16)
            return carry

        lax.fori_loop(0, n_ctx, restore, 0)

    def exchange(step):
        rows = pl.ds(step * chunk, chunk)
        return remote(
            part.at[rows],
            partner_part.at[rows],
            pair_send.at[step],
            pair_recv.at[step],
            "tensor",
            1 - core,
        )

    for step in range(n_ctx):
        rows = slice(step * chunk, (step + 1) * chunk)
        part[rows, :] = dot_nt(mixed_ref[rows, :], proj_ref[:, 3 * columns :]).astype(BF16)
        exchange(step).start()
    for step in range(n_ctx):
        rows = slice(step * chunk, (step + 1) * chunk)
        exchange(step).wait_recv()
        branch = part[rows, :].astype(F32) + partner_part[rows, :].astype(F32)
        first_in_ref[rows, :] = x_ref[rows, :].astype(F32) + (branch + output_bias)

    for step in range(n_ctx):
        exchange(step).wait_send()
    for pair in range(pairs):
        for hop in range(1, n_ctx):
            moved(pair, hop).wait_send()
            sent_back(pair, hop).wait_send()
    if gathers:
        for copy in gather_copies:
            copy.wait_send()
        for copy in feed_copies:
            copy.wait_send()
        own[4].wait()
        own[5].wait()
        for step in range(1, n_dp):
            source = lax.rem(dp - step + n_dp, n_dp)
            rows = pl.ds(pl.multiple_of(source * shard, 16), shard)
            remote(
                outer_full_ref.at[rows],
                outer_full_ref.at[rows],
                feed_send.at[step],
                feed_recv.at[source],
                "dp",
                source,
            ).wait_recv()
            for hop in range(1, n_ctx):
                other = partner(ctx, hop, n_ctx)
                remote(
                    strip(source, other),
                    strip(source, other),
                    inner_forward.at[step, hop],
                    inner_recv.at[other, source],
                    "context",
                    other,
                ).wait_recv()


def forward_attention(x, weights, cols, rows, biases, gathers):
    n_dp, n_ctx = lax.axis_size("dp"), lax.axis_size("context")
    slab, width = x.shape
    columns = weights[0].shape[1]
    hidden = weights[4].shape[1]
    pairs = columns // PAIR
    groups, share, chunk = slab // CLUSTER, CLUSTER // n_ctx, slab // n_ctx
    vmem = pl.BlockSpec(memory_space=pltpu.VMEM)
    hbm = pl.BlockSpec(memory_space=pl.ANY)
    dma = pltpu.SemaphoreType.DMA
    shapes = (
        jax.ShapeDtypeStruct((slab, width), F32),
        jax.ShapeDtypeStruct((slab, columns), BF16),
        jax.ShapeDtypeStruct((pairs, groups, CLUSTER, 3 * PAIR), BF16),
        jax.ShapeDtypeStruct((width, 4 * columns), BF16),
        jax.ShapeDtypeStruct((width, hidden), BF16),
        jax.ShapeDtypeStruct((width, hidden), BF16),
    )
    weight_spec = hbm if gathers else vmem
    return pl.pallas_call(
        functools.partial(forward_kernel, (n_dp, n_ctx, pairs, gathers)),
        out_shape=shapes,
        in_specs=[vmem] + [weight_spec] * 4 + [hbm] * 2 + [vmem] * 5,
        out_specs=(vmem, vmem, vmem, vmem, hbm, hbm),
        scratch_shapes=[
            pltpu.VMEM((pairs, slab, 3 * PAIR), BF16),
            pltpu.VMEM((pairs, n_ctx, groups, share, 3 * PAIR), BF16),
            pltpu.VMEM((pairs, groups, CLUSTER, PAIR), BF16),
            pltpu.VMEM((pairs, n_ctx, groups, share, PAIR), BF16),
            pltpu.VMEM((slab, width), BF16),
            pltpu.VMEM((slab, width), BF16),
            dma((6,)),
            dma((n_dp,)),
            dma((n_dp, n_ctx)),
            dma((4, n_dp)),
            dma((n_dp,)),
            dma((n_dp,)),
            dma((n_dp,)),
            dma((n_dp, n_ctx)),
            dma((n_ctx, n_dp)),
            dma((pairs, n_ctx)),
            dma((pairs, n_ctx)),
            dma((pairs, n_ctx)),
            dma((pairs, n_ctx)),
            dma((n_ctx,)),
            dma((n_ctx,)),
        ],
        compiler_params=pltpu.CompilerParams(collective_id=0, has_side_effects=True),
        name="forward_attention",
    )(x, *weights, cols, rows, *biases)


def store_chunk(ref, index, values):
    if len(ref.shape) == 3:
        ref[index] = values
        return
    n_ctx, n_dp, tile = ref.shape[1:4]
    for owner in range(n_dp):
        for place in range(n_ctx):
            row = (owner * n_ctx + place) * tile
            ref[index, place, owner] = values[row : row + tile]


def chunk_shape(count, width, columns, split):
    n_dp, n_ctx = lax.axis_size("dp"), lax.axis_size("context")
    if split:
        return (count, n_ctx, n_dp, width // (n_dp * n_ctx), columns)
    return (count, width, columns)


def sublane_sums(values):
    rows, width = values.shape
    return jnp.sum(values.reshape(rows // 8, 8, width), axis=0)


def feed_kernel(
    blocks,
    first_in_ref,
    cotangent_ref,
    inner_ref,
    outer_ref,
    inner_bias_ref,
    outer_bias_ref,
    first_gain_ref,
    first_shift_ref,
    second_gain_ref,
    second_shift_ref,
    activations_ref,
    summed_ref,
    branch_ref,
    inner_grad_ref,
    outer_grad_ref,
    sums_ref,
    low,
    first,
    act,
    slope,
    feed,
    part,
    partner_part,
    sums,
    pair_send,
    pair_recv,
):
    slab, width = first_in_ref.shape
    hidden = inner_ref.shape[1]
    chunk = slab // blocks
    core = lax.axis_index("tensor")
    meet(("tensor",))
    inner_bias, outer_bias = row_of(inner_bias_ref), row_of(outer_bias_ref)
    first_gain, first_shift = row_of(first_gain_ref), row_of(first_shift_ref)
    second_gain, second_shift = row_of(second_gain_ref), row_of(second_shift_ref)
    sums[...] = jnp.zeros_like(sums)

    def rows_of(step):
        return pl.ds(pl.multiple_of(step * chunk, chunk), chunk)

    def exchange(stage, step):
        return remote(
            part.at[stage, rows_of(step)],
            partner_part.at[stage, rows_of(step)],
            pair_send.at[stage, step],
            pair_recv.at[stage, step],
            "tensor",
            1 - core,
        )

    def expand(step, carry):
        rows = rows_of(step)
        normed, _ = normalize(first_in_ref[rows, :])
        values = normed * first_gain + first_shift
        first[rows, :] = values
        low[rows, :] = values.astype(BF16)
        inner = dot(low[rows, :], inner_ref[...]) + inner_bias
        cdf = 0.5 * (1.0 + lax.erf(inner * 0.7071067811865476))
        act[rows, :] = (inner * cdf).astype(BF16)
        slope[rows, :] = (
            cdf + inner * jnp.exp(-0.5 * inner * inner) * 0.3989422804014327
        ).astype(BF16)
        part[0, rows, :] = dot_nt(act[rows, :], outer_ref[...]).astype(BF16)
        exchange(0, step).start()
        return carry

    lax.fori_loop(0, blocks, expand, 0)

    def turn(step, carry):
        rows = rows_of(step)
        exchange(0, step).wait_recv()
        out = part[0, rows, :].astype(F32) + partner_part[0, rows, :].astype(F32)
        normed, root = normalize(first[rows, :] + (out + outer_bias))
        activations_ref[rows, :] = (
            normed * second_gain + second_shift
        ).astype(BF16)
        upstream = cotangent_ref[rows, :].astype(F32)
        grad = norm_backward(upstream, normed, root, second_gain)
        first[rows, :] = grad
        rounded = grad.astype(BF16)
        feed[rows, :] = rounded
        sums[2] += sublane_sums(rounded.astype(F32))
        sums[5] += sublane_sums(upstream * normed)
        sums[6] += sublane_sums(upstream)
        inner_grad = dot(rounded, outer_ref[...]) * slope[rows, :].astype(F32)
        slope[rows, :] = inner_grad.astype(BF16)
        inner_sums = sublane_sums(slope[rows, :].astype(F32))
        sums[0] += inner_sums[:, :width]
        sums[1] += inner_sums[:, width:]
        part[1, rows, :] = dot_nt(slope[rows, :], inner_ref[...]).astype(BF16)
        exchange(1, step).start()
        return carry

    lax.fori_loop(0, blocks, turn, 0)

    strip = hidden // blocks

    def weigh(step, carry):
        lanes = pl.ds(pl.multiple_of(step * strip, strip), strip)
        store_chunk(outer_grad_ref, step, dot_tn(feed[...], act[:, lanes]).astype(BF16))
        store_chunk(inner_grad_ref, step, dot_tn(low[...], slope[:, lanes]).astype(BF16))
        return carry

    lax.fori_loop(0, blocks, weigh, 0)

    def close(step, carry):
        rows = rows_of(step)
        exchange(1, step).wait_recv()
        back = part[1, rows, :].astype(F32) + partner_part[1, rows, :].astype(F32)
        grad = first[rows, :] + back
        normed, root = normalize(first_in_ref[rows, :])
        sums[3] += sublane_sums(grad * normed)
        sums[4] += sublane_sums(grad)
        summed = norm_backward(grad, normed, root, first_gain)
        summed_ref[rows, :] = summed
        rounded = summed.astype(BF16)
        branch_ref[rows, :] = rounded
        sums[7] += sublane_sums(rounded.astype(F32))
        return carry

    lax.fori_loop(0, blocks, close, 0)
    sums_ref[...] = jnp.sum(sums[...], axis=1)

    def finish(step, carry):
        exchange(0, step).wait_send()
        exchange(1, step).wait_send()
        return carry

    lax.fori_loop(0, blocks, finish, 0)


def feed_forward(first_in, cotangent, inner, outer, vectors, split):
    slab, width = first_in.shape
    hidden = inner.shape[1]
    blocks = lax.axis_size("context")
    vmem = pl.BlockSpec(memory_space=pltpu.VMEM)
    dma = pltpu.SemaphoreType.DMA
    return pl.pallas_call(
        functools.partial(feed_kernel, blocks),
        out_shape=(
            jax.ShapeDtypeStruct((slab, width), BF16),
            jax.ShapeDtypeStruct((slab, width), F32),
            jax.ShapeDtypeStruct((slab, width), BF16),
            jax.ShapeDtypeStruct(chunk_shape(blocks, width, hidden // blocks, split), BF16),
            jax.ShapeDtypeStruct(chunk_shape(blocks, width, hidden // blocks, split), BF16),
            jax.ShapeDtypeStruct((8, width), F32),
        ),
        in_specs=[vmem] * (4 + len(vectors)),
        out_specs=[vmem] * 6,
        scratch_shapes=[
            pltpu.VMEM((slab, width), BF16),
            pltpu.VMEM((slab, width), F32),
            pltpu.VMEM((slab, hidden), BF16),
            pltpu.VMEM((slab, hidden), BF16),
            pltpu.VMEM((slab, width), BF16),
            pltpu.VMEM((2, slab, width), BF16),
            pltpu.VMEM((2, slab, width), BF16),
            pltpu.VMEM((8, 8, width), F32),
            dma((2, blocks)),
            dma((2, blocks)),
        ],
        compiler_params=pltpu.CompilerParams(collective_id=1, has_side_effects=True),
        name="feed_forward",
    )(first_in, cotangent, inner, outer, *vectors)


def backward_kernel(
    sizes,
    x_ref,
    branch_ref,
    summed_ref,
    mixed_ref,
    got_ref,
    proj_ref,
    cols_ref,
    rows_ref,
    inner_part_ref,
    outer_part_ref,
    sums_ref,
    input_grad_ref,
    final_ref,
    totals_ref,
    proj_part_ref,
    upstream,
    sending,
    landed,
    answer,
    returned,
    restored,
    collected,
    pieces,
    gathered,
    part,
    partner_part,
    sums,
    sums_ctx,
    sums_dp,
    move_send,
    move_recv,
    back_send,
    back_recv,
    first_send,
    first_recv,
    second_send,
    second_recv,
    third_send,
    third_recv,
    sums_send,
    sums_recv,
    pair_send,
    pair_recv,
):
    n_dp, n_ctx, pairs, reduces = sizes
    slab, width = x_ref.shape
    columns = pairs * PAIR
    dp, ctx, core = lax.axis_index("dp"), lax.axis_index("context"), lax.axis_index("tensor")
    chunk = slab // n_ctx
    groups = slab // CLUSTER
    share = CLUSTER // n_ctx
    shard = width // n_dp
    meet(("dp", "context", "tensor") if reduces else ("context", "tensor"))

    def rows_of(step):
        return pl.ds(pl.multiple_of(step * chunk, chunk), chunk)

    strips = n_ctx
    half = strips // 2
    groups_of = [(proj_part_ref, number, 1, number, "context") for number in range(1 + pairs)]
    inner_near, inner_far, outer_far = range(1 + pairs, 4 + pairs)
    groups_of.append((inner_part_ref, 0, half, 1 + pairs, "context"))
    groups_of.append((inner_part_ref, half, strips - half, 1 + pairs + half, "dp"))
    groups_of.append((outer_part_ref, 0, strips, 1 + pairs + strips, "dp"))
    places = {"context": (n_ctx, ctx, "dp"), "dp": (n_dp, dp, "context")}

    def first(group, hop):
        source, start, count, chunk, axis = groups_of[group]
        size, own, _ = places[axis]
        target = peer(axis, own, hop, size)
        if axis == "context":
            sent = source.at[start : start + count, target]
        else:
            sent = source.at[start : start + count, :, target]
        landing = collected.at[hop, chunk : chunk + count]
        if hop == 0:
            return pltpu.make_async_copy(sent, landing, first_recv.at[group, 0])
        return remote(
            sent, landing, first_send.at[group, hop], first_recv.at[group, hop], axis, target
        )

    def second(group, hop):
        _, _, count, chunk, axis = groups_of[group]
        other = places[axis][2]
        size, own, _ = places[other]
        target = peer(other, own, hop, size)
        return remote(
            pieces.at[chunk : chunk + count, target],
            gathered.at[hop, chunk : chunk + count],
            second_send.at[group, hop],
            second_recv.at[group, hop],
            other,
            target,
        )

    def third(group, hop, mine):
        _, _, count, chunk, _ = groups_of[group]
        owner = ctx if mine else partner(ctx, hop, n_ctx)
        block = final_ref.at[chunk : chunk + count, owner]
        return remote(
            block,
            block,
            third_send.at[group, hop],
            third_recv.at[group, hop],
            "context",
            partner(ctx, hop, n_ctx),
        )

    def first_size(group):
        return places[groups_of[group][4]][0]

    def second_size(group):
        return places[places[groups_of[group][4]][2]][0]

    def start_first(group):
        for hop in (*range(1, first_size(group)), 0):
            first(group, hop).start()

    def sum_first(group):
        _, _, count, chunk, _ = groups_of[group]
        first(group, 0).wait()
        for hop in range(1, first_size(group)):
            first(group, hop).wait_recv()

        def add(step, carry):
            total = collected[0, chunk + step].astype(F32)
            for hop in range(1, first_size(group)):
                total = total + collected[hop, chunk + step].astype(F32)
            pieces[chunk + step] = total.astype(BF16)
            return carry

        lax.fori_loop(0, count, add, 0)
        for hop in range(1, second_size(group)):
            second(group, hop).start()

    def sum_second(group):
        _, _, count, chunk, axis = groups_of[group]
        own = places[places[axis][2]][1]
        for hop in range(1, second_size(group)):
            second(group, hop).wait_recv()
        for number in range(chunk, chunk + count):
            total = pieces[number, own].astype(F32)
            for hop in range(1, second_size(group)):
                total = total + gathered[hop, number].astype(F32)
            final_ref[number, ctx] = total.astype(BF16)
        for hop in range(1, n_ctx):
            third(group, hop, True).start()

    if reduces:
        start_first(outer_far)
        start_first(inner_far)

    def project(step, carry):
        rows = rows_of(step)
        upstream[rows, :] = dot(branch_ref[rows, :], proj_ref[:, 3 * columns :]).astype(BF16)
        return carry

    lax.fori_loop(0, n_ctx, project, 0)

    own_share = pl.ds(pl.multiple_of(ctx * share, share), share)

    def moved(pair, hop):
        target = partner(ctx, hop, n_ctx)
        source = sending.at[pair, target]
        landing = landed.at[pair, :, own_share, :]
        if hop == 0:
            return pltpu.make_async_copy(source, landing, move_recv.at[pair, 0])
        return remote(
            source, landing, move_send.at[pair, hop], move_recv.at[pair, hop], "context", target
        )

    for pair in range(pairs):
        for hop in (*range(1, n_ctx), 0):
            target = partner(ctx, hop, n_ctx)
            rows = rows_of(target)
            positions = lax.broadcasted_iota(jnp.int32, (chunk, slab), 1)
            values = upstream[:, pair * PAIR : (pair + 1) * PAIR]
            even = dot(one_hot(cols_ref[rows, 2 * pair : 2 * pair + 1], positions), values)
            odd = dot(one_hot(cols_ref[rows, 2 * pair + 1 : 2 * pair + 2], positions), values)
            picked = jnp.where(low_lanes(even.shape), even, odd).astype(BF16)
            sending[pair, target] = picked.reshape(groups, share, PAIR)
            moved(pair, hop).start()

    if reduces:
        start_first(inner_near)
    store_chunk(proj_part_ref, 0, dot_tn(branch_ref[...], mixed_ref[...]).astype(BF16))
    if reduces:
        start_first(0)

    def sent_back(pair, hop):
        target = partner(ctx, hop, n_ctx)
        rows = pl.ds(pl.multiple_of(target * share, share), share)
        source = answer.at[pair, :, rows, :]
        landing = returned.at[pair, ctx]
        if hop == 0:
            return pltpu.make_async_copy(source, landing, back_recv.at[pair, 0])
        return remote(
            source, landing, back_send.at[pair, hop], back_recv.at[pair, hop], "context", target
        )

    for pair in range(pairs):
        for hop in range(n_ctx):
            copy = moved(pair, hop)
            if hop == 0:
                copy.wait()
            else:
                copy.wait_recv()

        def attend(group, carry):
            query2 = stack_pair(got_ref[pair, group, :, 0:PAIR])
            key = got_ref[pair, group, :, PAIR : 2 * PAIR]
            value = got_ref[pair, group, :, 2 * PAIR : 3 * PAIR]
            grad2 = stack_pair(landed[pair, group])
            masks = pair_mask(cols_ref, rows_ref, pair, group, 2 * pairs)
            raw = dot_nt(query2, key) * HEAD_DIM ** (-0.5)
            scores = jnp.concatenate(
                [
                    jnp.where(mask, raw[i * CLUSTER : (i + 1) * CLUSTER], masked_score)
                    for i, mask in enumerate(masks)
                ],
                axis=0,
            )
            exponent = jnp.exp(scores - jnp.max(scores, axis=1, keepdims=True))
            probs = exponent / jnp.sum(exponent, axis=1, keepdims=True)
            prob_grad = dot_nt(grad2, value)
            inner = jnp.sum(probs * prob_grad, axis=1, keepdims=True)
            score_grad = (probs * (prob_grad - inner) * HEAD_DIM ** (-0.5)).astype(BF16)
            value_grad = dot_tn(probs.astype(BF16), grad2)
            query_grad = fold_pair(dot(score_grad, key))
            key_grad = dot_tn(score_grad, query2)
            low = low_lanes((CLUSTER, PAIR))
            first = jnp.where(low, query_grad, pltpu.roll(key_grad, HEAD_DIM, 1))
            second = jnp.where(low, pltpu.roll(query_grad, HEAD_DIM, 1), key_grad)
            answer[pair, group, :, 0:PAIR] = first.astype(BF16)
            answer[pair, group, :, PAIR : 2 * PAIR] = second.astype(BF16)
            answer[pair, group, :, 2 * PAIR : 3 * PAIR] = value_grad.astype(BF16)
            return carry

        lax.fori_loop(0, groups, attend, 0, unroll=2)
        for hop in (*range(1, n_ctx), 0):
            sent_back(pair, hop).start()

    if reduces:
        sum_first(0)
    for pair in range(pairs):
        for hop in range(n_ctx):
            copy = sent_back(pair, hop)
            if hop == 0:
                copy.wait()
            else:
                copy.wait_recv()

        def restore(step, carry):
            rows = rows_of(step)
            positions = lax.broadcasted_iota(jnp.int32, (chunk, slab), 0) + step * chunk
            values = returned[pair].reshape(slab, 3 * PAIR)
            shared = values[:, 2 * PAIR :]
            even = dot(
                one_hot(rows_ref[2 * pair : 2 * pair + 1, :], positions),
                jnp.concatenate((values[:, :PAIR], shared), axis=1),
            )
            odd = dot(
                one_hot(rows_ref[2 * pair + 1 : 2 * pair + 2, :], positions), values[:, PAIR:]
            )
            low = low_lanes((chunk, PAIR))
            first, second = even[:, :PAIR], odd[:, :PAIR]
            query = jnp.where(low, first, pltpu.roll(second, HEAD_DIM, 1))
            key = jnp.where(low, pltpu.roll(first, HEAD_DIM, 1), second)
            value = jnp.where(low, even[:, PAIR:], odd[:, PAIR:])
            for number, piece in enumerate((query, key, value)):
                lanes = slice(number * columns + pair * PAIR, number * columns + (pair + 1) * PAIR)
                restored[rows, lanes] = piece.astype(BF16)
            return carry

        lax.fori_loop(0, n_ctx, restore, 0)
        grads = jnp.concatenate(
            [
                restored[:, number * columns + pair * PAIR : number * columns + (pair + 1) * PAIR]
                for number in range(3)
            ],
            axis=1,
        )
        store_chunk(proj_part_ref, 1 + pair, dot_tn(x_ref[...], grads).astype(BF16))
        if reduces:
            start_first(1 + pair)

    def exchange(step):
        return remote(
            part.at[rows_of(step)],
            partner_part.at[rows_of(step)],
            pair_send.at[step],
            pair_recv.at[step],
            "tensor",
            1 - core,
        )

    def give(step, carry):
        rows = rows_of(step)
        part[rows, :] = dot_nt(restored[rows, :], proj_ref[:, : 3 * columns]).astype(BF16)
        exchange(step).start()
        return carry

    lax.fori_loop(0, n_ctx, give, 0)

    sums[0:8, :] = sums_ref[...]
    sums[8:16, :] = jnp.zeros((8, width), F32)
    for place, number in enumerate((0, 2)):
        values = restored[:, number * columns : (number + 1) * columns].astype(F32)
        sums[8:9, place * columns : (place + 1) * columns] = jnp.sum(values, axis=0, keepdims=True)

    def sums_out(level, step):
        axis, size, own = (("context", n_ctx, ctx), ("dp", n_dp, dp))[level]
        landing = (sums_ctx, sums_dp)[level]
        return remote(
            sums.at[level * 16 : level * 16 + 16],
            landing.at[own],
            sums_send.at[level, step],
            sums_recv.at[level, step],
            axis,
            lax.rem(own + step, size),
        )

    if reduces:
        for step in range(1, n_ctx):
            sums_out(0, step).start()
        sums_ctx[ctx] = sums[0:16, :]

    def take(step, carry):
        rows = rows_of(step)
        exchange(step).wait_recv()
        back = part[rows, :].astype(F32) + partner_part[rows, :].astype(F32)
        input_grad_ref[rows, :] = (summed_ref[rows, :] + back).astype(BF16)
        return carry

    if reduces:
        sum_first(outer_far)
        sum_first(inner_near)
    lax.fori_loop(0, n_ctx, take, 0)

    if reduces:
        for step in range(1, n_ctx):
            sums_out(0, step).wait_recv()
        sums[16:32, :] = jnp.sum(sums_ctx[...], axis=0)
        for step in range(1, n_dp):
            sums_out(1, step).start()
        sums_dp[dp] = sums[16:32, :]
        for pair in range(pairs - 1):
            sum_first(1 + pair)
        sum_first(inner_far)
        sum_first(pairs)
        sum_second(outer_far)
        sum_second(0)
        sum_second(inner_near)
        for step in range(1, n_dp):
            sums_out(1, step).wait_recv()
        totals_ref[...] = jnp.sum(sums_dp[...], axis=0)
        for pair in range(pairs - 1):
            sum_second(1 + pair)
        sum_second(inner_far)
        sum_second(pairs)
        for group in range(4 + pairs):
            for hop in range(1, n_ctx):
                third(group, hop, False).wait_recv()
            for hop in range(1, n_ctx):
                third(group, hop, True).wait_send()
            for hop in range(1, first_size(group)):
                first(group, hop).wait_send()
            for hop in range(1, second_size(group)):
                second(group, hop).wait_send()
        for level, size in enumerate((n_ctx, n_dp)):
            for step in range(1, size):
                sums_out(level, step).wait_send()
    else:
        totals_ref[...] = sums[0:16, :]
    for step in range(n_ctx):
        exchange(step).wait_send()
    for pair in range(pairs):
        for hop in range(1, n_ctx):
            moved(pair, hop).wait_send()
            sent_back(pair, hop).wait_send()


def backward_attention(
    x, branch, summed, mixed, got, proj, cols, rows, inner_part, outer_part, sums, reduces
):
    n_dp, n_ctx = lax.axis_size("dp"), lax.axis_size("context")
    slab, width = x.shape
    columns = mixed.shape[1]
    pairs = columns // PAIR
    groups, share = slab // CLUSTER, CLUSTER // n_ctx
    shard = width // n_dp
    vmem = pl.BlockSpec(memory_space=pltpu.VMEM)
    hbm = pl.BlockSpec(memory_space=pl.ANY)
    dma = pltpu.SemaphoreType.DMA
    chunks, steps = (1 + pairs + 2 * n_ctx, n_dp) if reduces else (1, 1)
    tile = shard // n_ctx if reduces else 16
    total = 4 + pairs
    hops = max(n_ctx, steps)
    return pl.pallas_call(
        functools.partial(backward_kernel, (n_dp, n_ctx, pairs, reduces)),
        out_shape=(
            jax.ShapeDtypeStruct((slab, width), BF16),
            jax.ShapeDtypeStruct((chunks, n_ctx, tile, columns), BF16),
            jax.ShapeDtypeStruct((16, width), F32),
            jax.ShapeDtypeStruct(chunk_shape(1 + pairs, width, columns, reduces), BF16),
        ),
        in_specs=[vmem] * 8 + [hbm] * 2 + [vmem],
        out_specs=[vmem] * 4,
        scratch_shapes=[
            pltpu.VMEM((slab, columns), BF16),
            pltpu.VMEM((pairs, n_ctx, groups, share, PAIR), BF16),
            pltpu.VMEM((pairs, groups, CLUSTER, PAIR), BF16),
            pltpu.VMEM((pairs, groups, CLUSTER, 3 * PAIR), BF16),
            pltpu.VMEM((pairs, n_ctx, groups, share, 3 * PAIR), BF16),
            pltpu.VMEM((slab, 3 * columns), BF16),
            pltpu.VMEM((hops, chunks, n_ctx, tile, columns), BF16),
            pltpu.VMEM((chunks, n_ctx, tile, columns), BF16),
            pltpu.VMEM((hops, chunks, tile, columns), BF16),
            pltpu.VMEM((slab, width), BF16),
            pltpu.VMEM((slab, width), BF16),
            pltpu.VMEM((32, width), F32),
            pltpu.VMEM((n_ctx, 16, width), F32),
            pltpu.VMEM((steps, 16, width), F32),
            dma((pairs, n_ctx)),
            dma((pairs, n_ctx)),
            dma((pairs, n_ctx)),
            dma((pairs, n_ctx)),
            dma((total, hops)),
            dma((total, hops)),
            dma((total, hops)),
            dma((total, hops)),
            dma((total, hops)),
            dma((total, hops)),
            dma((2, hops)),
            dma((2, hops)),
            dma((n_ctx,)),
            dma((n_ctx,)),
        ],
        compiler_params=pltpu.CompilerParams(collective_id=2, has_side_effects=True),
        name="backward_attention",
    )(x, branch, summed, mixed, got, proj, cols, rows, inner_part, outer_part, sums)


def results_kernel(
    activations_in,
    input_grad_in,
    final_ref,
    totals_ref,
    activations_ref,
    input_grad_ref,
    query_ref,
    key_ref,
    value_ref,
    output_ref,
    inner_ref,
    outer_ref,
    query_bias_ref,
    value_bias_ref,
    output_bias_ref,
    inner_bias_ref,
    outer_bias_ref,
    first_gain_ref,
    first_shift_ref,
    second_gain_ref,
    second_shift_ref,
):
    chunks, blocks, tile, columns = final_ref.shape
    width = totals_ref.shape[1]
    pairs = columns // PAIR
    strips = (chunks - 1 - pairs) // 2
    activations_ref[...] = activations_in[...]
    input_grad_ref[...] = input_grad_in[...]
    for block in range(blocks):
        rows = slice(block * tile, (block + 1) * tile)
        output_ref[rows, :] = final_ref[0, block].astype(F32)
        for pair in range(pairs):
            lanes = slice(pair * PAIR, (pair + 1) * PAIR)
            for number, ref in enumerate((query_ref, key_ref, value_ref)):
                part = final_ref[1 + pair, block, :, number * PAIR : (number + 1) * PAIR]
                ref[rows, lanes] = part.astype(F32)
        for number, ref in enumerate((inner_ref, outer_ref)):
            for strip in range(strips):
                lanes = slice(strip * columns, (strip + 1) * columns)
                chunk = 1 + pairs + number * strips + strip
                ref[rows, lanes] = final_ref[chunk, block].astype(F32)
    query_bias_ref[...] = totals_ref[8, :columns]
    value_bias_ref[...] = totals_ref[8, columns:]
    output_bias_ref[...] = totals_ref[7, :]
    inner_bias_ref[:width] = totals_ref[0, :]
    inner_bias_ref[width:] = totals_ref[1, :]
    rest = (outer_bias_ref, first_gain_ref, first_shift_ref, second_gain_ref, second_shift_ref)
    for number, ref in enumerate(rest):
        ref[...] = totals_ref[2 + number, :]


def write_results(activations, input_grad, final, totals):
    chunks, blocks, tile, columns = final.shape
    slab, width = activations.shape
    shard = blocks * tile
    hidden = (chunks - 1 - columns // PAIR) // 2 * columns
    shapes = (
        [(shard, columns)] * 4
        + [(shard, hidden)] * 2
        + [(columns,)] * 2
        + [(width,), (hidden,)]
        + [(width,)] * 5
    )
    vmem = pl.BlockSpec(memory_space=pltpu.VMEM)
    results = pl.pallas_call(
        results_kernel,
        out_shape=[jax.ShapeDtypeStruct((slab, width), BF16)] * 2
        + [jax.ShapeDtypeStruct(shape, F32) for shape in shapes],
        in_specs=[vmem] * 4,
        out_specs=[vmem] * 17,
        name="write_results",
    )(activations, input_grad, final, totals)
    activations, input_grad, query, key, value, output, inner, outer = results[:8]
    return (
        activations[None],
        input_grad[None],
        query,
        key,
        value,
        output.T,
        inner,
        outer.T,
        *results[8:],
    )


def slot_tables(cluster_order, prefix_length, own, n_ctx):
    heads, length = cluster_order.shape[1:]
    slab = length // n_ctx
    order = cluster_order.reshape(heads, n_ctx, slab // CLUSTER, n_ctx, CLUSTER // n_ctx)
    rows = lax.dynamic_index_in_dim(order, own, axis=3, keepdims=False).reshape(heads, slab)
    rows = rows - own * slab
    places = lax.dynamic_slice_in_dim(cluster_order[0], own * slab, slab, axis=1)
    gap = jnp.zeros((8 - heads % 8, slab), jnp.int32)
    limits = jnp.maximum(places, prefix_length[0] - 1)
    along = jnp.concatenate((rows, gap, places, gap), axis=0)
    down = jnp.concatenate((rows, gap, limits, gap), axis=0).T
    return down, along


def shards(
    tokens,
    prefix_length,
    cluster_order,
    query_weight,
    key_weight,
    value_weight,
    output_weight,
    inner_weight,
    outer_weight,
    query_bias,
    value_bias,
    output_bias,
    inner_bias,
    outer_bias,
    first_gain,
    first_shift,
    second_gain,
    second_shift,
    cotangent,
):
    n_ctx = lax.axis_size("context")
    own = lax.axis_index("context")
    x = tokens[0]
    shard, columns = query_weight.shape
    aligned = n_ctx == lax.axis_size("dp") and shard % (16 * n_ctx) == 0
    weights = (query_weight, key_weight, value_weight, output_weight.T, inner_weight, outer_weight.T)
    if not aligned:
        weights = tuple(lax.all_gather(w, "dp", axis=0, tiled=True) for w in weights)
    cols, rows = slot_tables(cluster_order, prefix_length, own, n_ctx)
    biases = (query_bias, value_bias, output_bias)
    vectors = (inner_bias, outer_bias, first_gain, first_shift, second_gain, second_shift)
    first_in, mixed, got, proj, inner_full, outer_full = forward_attention(
        x, weights, cols, rows, biases, aligned
    )
    if not aligned:
        inner_full, outer_full = weights[4:]
    activations, summed, branch, inner_part, outer_part, sums = feed_forward(
        first_in, cotangent[0], inner_full, outer_full, vectors, aligned
    )
    input_grad, final, totals, proj_part = backward_attention(
        x, branch, summed, mixed, got, proj, cols, rows, inner_part, outer_part, sums, aligned
    )
    if not aligned:
        parts = jnp.concatenate((proj_part, inner_part, outer_part), axis=0)
        piece = lax.psum_scatter(parts, "dp", scatter_dimension=1, tiled=True)
        final = lax.psum(piece, "context")[:, None]
        totals = lax.psum(totals, ("dp", "context"))
    return write_results(activations, input_grad, final, totals)


def solution(mesh):
    placed = (
        P("dp", "context", None),
        P("dp"),
        P("dp", "tensor", None),
        P("dp", "tensor"),
        P("dp", "tensor"),
        P("dp", "tensor"),
        P("tensor", "dp"),
        P("dp", "tensor"),
        P("tensor", "dp"),
        P("tensor"),
        P("tensor"),
        P(),
        P("tensor"),
        P(),
        P(),
        P(),
        P(),
        P(),
        P("dp", "context", None),
    )
    return jax.shard_map(
        shards,
        mesh=mesh,
        in_specs=placed,
        out_specs=(
            P("dp", "context", None),
            P("dp", "context", None),
            P("dp", "tensor"),
            P("dp", "tensor"),
            P("dp", "tensor"),
            P("tensor", "dp"),
            P("dp", "tensor"),
            P("tensor", "dp"),
            P("tensor"),
            P("tensor"),
            P(),
            P("tensor"),
            P(),
            P(),
            P(),
            P(),
            P(),
        ),
        check_vma=False,
    )
```
